128 devices in a mesh: attn: 4 (over z_hi, core), exp: 32 (over z_lo, y, x).
Axes of the slice: x: 4, y: 4, z: 4 (z_hi: 2, z_lo: 2; z = z_hi * 2 + z_lo), core: 2. Of those that a mesh axis runs over, the one named last changes fastest.
Arguments:
- tokens: bfloat16 [2, 1024, 7168], P(None, 'exp', 'attn'), may hold values from -6 to 6
- logits: float32 [2, 1024, 8], P(None, 'exp'), may hold values from -8 to 8
- routes: int32 [2, 1024, 8], P(None, 'exp'), may hold values from 0 to 31, all different within a row; in each aligned block of 32 rows (0 to 31, 32 to 63, ..., all dimensions but the last counted through in order) at most 16 rows name the same one
- held: int32 [32], replicated, may hold values from 0 to 31, each once
- swapped: int32 [16], replicated, may hold values 0 or 1
- w_gate: bfloat16 [32, 7168, 1024], P('exp', None, 'attn'), may hold values from -0.0625 to 0.0625
- w_up: bfloat16 [32, 7168, 1024], P('exp', None, 'attn'), may hold values from -0.0625 to 0.0625
- w_down: bfloat16 [32, 1024, 7168], P('exp', None, 'attn'), may hold values from -0.1875 to 0.1875
Outputs:
- mixed: bfloat16 [2, 1024, 7168], P(None, 'exp', 'attn')
- gate_after: bfloat16 [32, 7168, 1024], P('exp', None, 'attn')
- up_after: bfloat16 [32, 7168, 1024], P('exp', None, 'attn')
- down_after: bfloat16 [32, 1024, 7168], P('exp', None, 'attn')
The draws below stay inside these ranges and needn't reach their ends.
Inputs may be any that keep to these rules, and one draw needn't show every extreme that they name: `routes`: each row names 8 different experts; in each step, no expert is named by more than 16 rows of one index of exp, and some expert by exactly that many in some of them. `held`: each expert id once.
All inputs are finite; a program needn't handle non-finite values.
Results may differ from the reference program's by a relative error of at most 0.0058.
Values may be sent and summed in bfloat16 or wider, within the bound.
A program may use at most 128 MiB of HBM per device.

```python
import math
import jax
import jax.numpy as jnp
import numpy as np
from jax import lax

D = 7168
FF = 1024
TOP = 8
STEPS = 2
TOK_DEV = 32
EXPERTS = 32
CAP = 16
ROWS = 1024
N_EXP = 32


def set_ends(array, key, least, top_value):
    shape = array.shape
    place = [jax.random.randint(jax.random.fold_in(key, axis), (), 0, shape[axis]) for axis in range(len(shape))]
    array = array.at[tuple(place)].set(least)
    longest = shape.index(max(shape))
    place[longest] = (place[longest] + 1) % shape[longest]
    return array.at[tuple(place)].set(top_value)


def levels(stream_key, extent, cuts, smallest, top_value):
    def one(dim, blocks):
        draws = jax.random.uniform(jax.random.fold_in(jax.random.fold_in(stream_key, 6), dim), (blocks,), jnp.float32, smallest / len(cuts), top_value / len(cuts))
        return jnp.repeat(jnp.exp(draws), extent[dim] // blocks).reshape((-1,) + (1,) * (len(extent) - dim - 1))

    gain = one(*cuts[0])
    for cut in cuts[1:]:
        gain = gain * one(*cut)
    return gain


def assign_block(rng, own, number, rows, amount, top, bound, lean):
    ranking = jax.random.permutation(rng, amount)
    crowded, common = shares(amount, rows * top, bound, lean, True), shares(amount, rows * top, bound, lean, False)
    places = jnp.arange(amount)

    def named(tallies, offset_by):
        used = int((tallies > 0).sum())
        fixed = max(1, used // 4)
        shifted = fixed + (places - fixed + offset_by * (used - fixed)) % max(1, amount - fixed)
        return jnp.zeros((amount,), jnp.int32).at[ranking[jnp.where(places < fixed, places, shifted)]].set(jnp.asarray(tallies, jnp.int32))

    tallies = jnp.where(number % 4 == 0, named(crowded, number // 4), named(common, number - number // 4 - 1))
    mixed = jax.random.permutation(jax.random.fold_in(own, 3), amount)
    donor, sink = mixed[0:amount // 2 * 2:2], mixed[1:amount // 2 * 2:2]
    room = jnp.minimum(tallies[donor] - 1, bound - tallies[sink]) // 2
    room = jnp.where((donor == ranking[0]) | (sink == ranking[0]) | (tallies[sink] == 0), 0, jnp.maximum(room, 0))
    shifted = jax.random.randint(jax.random.fold_in(own, 4), (amount // 2,), 0, 1 << 20) % (room + 1)
    tallies = tallies.at[donor].add(-shifted).at[sink].add(shifted)
    members = jnp.searchsorted(jnp.cumsum(tallies), jnp.arange(rows * top), side="right").astype(jnp.int32)
    table = members.reshape(top, rows).T
    table = table[jax.random.permutation(jax.random.fold_in(own, 1), rows)]
    offset_by = jax.random.randint(jax.random.fold_in(own, 2), (rows, 1), 0, top)
    return jnp.take_along_axis(table, (jnp.arange(top)[None, :] + offset_by) % top, axis=1)


def shares(amount, total, reach, skew, full):
    weights = [(1 << 20) // math.isqrt(standing ** skew) + 1 for standing in range(1, amount + 1)]
    largest = reach if full else min(reach, max(-(-total // amount), total * weights[0] // sum(weights)))
    least = 1 if total - largest >= amount - 1 else 0
    given, surplus = [largest] + [least] * (amount - 1), total - largest - least * (amount - 1)
    while surplus > 0:
        candidates = [i for i in range(1, amount) if given[i] < largest] or [i for i in range(1, amount) if given[i] < reach]
        pool, remaining = sum([weights[i] for i in candidates]), surplus
        for i in candidates:
            addition = min(reach - given[i], max(1, remaining * weights[i] // pool), surplus)
            given[i] = given[i] + addition
            surplus = surplus - addition
    return np.array(given)


def normal_values(stream_key, extent, spread, most, cuts=(), held_as=jnp.bfloat16):
    result = spread * jax.random.normal(stream_key, extent, jnp.float32)
    if cuts:
        result = result * levels(stream_key, extent, cuts, -0.22, 0.18)
    return jnp.clip(result, -most, most).astype(held_as)


def setup_inputs(seed: int = 0) -> dict:
    key_list = jax.random.split(jax.random.key(seed), 9)
    tokens = normal_values(key_list[0], (STEPS, ROWS, D), 1.0, 6.0, ((1, 32), (2, 4)))
    logits = normal_values(key_list[1], (STEPS, ROWS, TOP), 2.0, 8.0, ((1, 32),), jnp.float32)
    routes_keys = jax.random.split(jax.random.fold_in(key_list[2], 1), STEPS * ROWS // TOK_DEV)
    routes_turns = jax.random.permutation(jax.random.fold_in(key_list[2], 3), STEPS * ROWS // TOK_DEV)
    routes = jax.vmap(lambda own, number: assign_block(jax.random.fold_in(key_list[2], 2), own, number, TOK_DEV, EXPERTS, TOP, CAP, 2))(routes_keys, routes_turns).reshape((STEPS, ROWS, TOP))
    held = jax.random.permutation(key_list[3], EXPERTS).astype(jnp.int32)
    swapped = set_ends((jax.random.randint(key_list[4], (EXPERTS // 2,), 0, 2) < 1).astype(jnp.int32), jax.random.fold_in(key_list[4], 1), 0, 1)
    w_gate = normal_values(key_list[5], (EXPERTS, D, FF), D ** -0.5, 0.0625, ((0, 32), (2, 4)))
    w_up = normal_values(key_list[6], (EXPERTS, D, FF), D ** -0.5, 0.0625, ((0, 32), (2, 4)))
    w_down = normal_values(key_list[7], (EXPERTS, FF, D), FF ** -0.5, 0.1875, ((0, 32), (2, 4)))
    return {"tokens": tokens, "logits": logits, "routes": routes, "held": held, "swapped": swapped, "w_gate": w_gate, "w_up": w_up, "w_down": w_down}


def reference(tokens, logits, routes, held, swapped, w_gate, w_up, w_down):
    half_count = N_EXP // 2
    devices = jnp.arange(N_EXP, dtype=jnp.int32)
    flags = swapped[devices % half_count]
    source = jnp.where(flags == 1, jnp.bitwise_xor(devices, half_count), devices)
    gate_after = w_gate[source]
    up_after = w_up[source]
    down_after = w_down[source]
    expert_ids = jnp.arange(EXPERTS, dtype=jnp.int32)
    tile_of = jnp.sum((held[None, :] == expert_ids[:, None]).astype(jnp.int32) * devices[None, :], axis=1)
    outputs = []
    for step in range(STEPS):
        chosen = routes[step].reshape(N_EXP, TOK_DEV * TOP)
        onehot = (chosen[:, :, None] == expert_ids[None, None, :]).astype(jnp.int32)
        slots = jnp.sum(jnp.cumsum(onehot, axis=1) * onehot, axis=2) - 1
        places = ((chosen * N_EXP + devices[:, None]) * CAP + slots).reshape(-1).astype(jnp.int32)
        row_ids = (jnp.arange(ROWS * TOP, dtype=jnp.int32) // TOP).astype(jnp.int32)
        table = jnp.full((EXPERTS * N_EXP * CAP,), ROWS, dtype=jnp.int32).at[places].set(row_ids)
        padded = jnp.concatenate([tokens[step], jnp.zeros((1, D), tokens.dtype)], axis=0)

        def serve(expert):
            tile = tile_of[expert]
            picks = lax.dynamic_slice_in_dim(table, (expert * (N_EXP * CAP)).astype(jnp.int32), N_EXP * CAP)
            rows = padded[picks]
            gate = jnp.dot(rows, w_gate[tile], preferred_element_type=jnp.float32)
            upper = jnp.dot(rows, w_up[tile], preferred_element_type=jnp.float32)
            hidden = (jax.nn.silu(gate) * upper).astype(jnp.bfloat16)
            return jnp.dot(hidden, w_down[tile], preferred_element_type=jnp.float32).astype(jnp.bfloat16)

        served = lax.map(serve, expert_ids)
        picked = served.reshape(-1, D)[places].reshape(ROWS, TOP, D).astype(jnp.float32)
        score = jax.nn.sigmoid(logits[step])
        weight = score / jnp.sum(score, axis=-1, keepdims=True)
        outputs.append((2.5 * jnp.sum(weight[:, :, None] * picked, axis=1)).astype(jnp.bfloat16))
    return jnp.stack(outputs, axis=0), gate_after, up_after, down_after
```

```python
import jax
import jax.numpy as jnp
from jax import lax
from jax.experimental import pallas as pl
from jax.experimental.pallas import tpu as pltpu
from jax.sharding import PartitionSpec as P

RING = 4


def wrap(value):
    return lax.rem(value + RING, RING)


def place():
    attn = lax.axis_index("attn")
    exp = lax.axis_index("exp")
    z_hi, core = attn // 2, lax.rem(attn, 2)
    z_lo, y, x = exp // 16, lax.rem(exp // 4, 4), lax.rem(exp, 4)
    return z_hi, core, z_lo, y, x


def device(z_hi, core, z_lo, y, x):
    return {"attn": z_hi * 2 + core, "exp": z_lo * 16 + y * 4 + x}


def neighbours(z_hi, core, z_lo, y, x):
    z = z_hi * 2 + z_lo
    right_z, left_z = wrap(z + 1), wrap(z - 1)
    along_z = [device(n // 2, core, lax.rem(n, 2), y, x) for n in (right_z, left_z)]
    along_x = [device(z_hi, core, z_lo, y, n) for n in (wrap(x + 1), wrap(x - 1))]
    along_y = [device(z_hi, core, z_lo, n, x) for n in (wrap(y + 1), wrap(y - 1))]
    return along_z, along_x, along_y, device(z_hi, 1 - core, z_lo, y, x)


def greet(devices):
    barrier = pltpu.get_barrier_semaphore()
    for other in devices:
        pl.semaphore_signal(barrier, inc=1, device_id=other, device_id_type=pl.DeviceIdType.MESH)
    pl.semaphore_wait(barrier, len(devices))


class Sends:
    def __init__(self, send_sem, recv_sem):
        self.send_sem, self.recv_sem, self.copies = send_sem, recv_sem, []

    def __call__(self, src, dst, to):
        k = len(self.copies)
        copy = pltpu.make_async_remote_copy(
            src_ref=src,
            dst_ref=dst,
            send_sem=self.send_sem.at[k],
            recv_sem=self.recv_sem.at[k],
            device_id=to,
            device_id_type=pl.DeviceIdType.MESH,
        )
        copy.start()
        self.copies.append(copy)
        return copy


GATHER_COPIES = 6 + 12 + 12 + 16


def gather_kernel(tok_ref, all_ref, local_sem, send_sem, recv_sem):
    z_hi, core, z_lo, y, x = place()
    along_z, along_x, along_y, sibling = neighbours(z_hi, core, z_lo, y, x)
    greet(along_z + along_x + along_y + [sibling])
    z = z_hi * 2 + z_lo
    quarter = tok_ref.shape[2]
    send = Sends(send_sem, recv_sem)

    def cols(high):
        return pl.ds(pl.multiple_of((high * 2 + core) * quarter, 128), quarter)

    def spot(step, at):
        return all_ref.at[step, lax.rem(at, 2), y, x, :, cols(at // 2)]

    own = [pltpu.make_async_copy(tok_ref.at[s], spot(s, z), local_sem.at[s]) for s in range(2)]
    for copy in own:
        copy.start()
    first = {}
    for s in range(2):
        for d in range(2):
            first[d, s] = send(tok_ref.at[s], spot(s, z), along_z[d])
    first[0, 0].wait_recv()
    forward0 = send(spot(0, wrap(z - 1)), spot(0, wrap(z - 1)), along_z[0])
    first[1, 1].wait_recv()
    forward1 = send(spot(1, wrap(z + 1)), spot(1, wrap(z + 1)), along_z[1])
    rest = {0: [first[1, 0], forward0], 1: [first[0, 1], forward1]}

    def line(step, axis, at, high):
        if axis == "x":
            return all_ref.at[step, :, y, at, :, cols(high)]
        return all_ref.at[step, :, at, x, :, cols(high)]

    def sheet(step, axis, at, high):
        if axis == "x":
            return all_ref.at[step, :, :, at, :, cols(high)]
        return all_ref.at[step, :, at, :, :, cols(high)]

    along = {"x": along_x, "y": along_y}
    spot_on = {"x": x, "y": y}
    order = (("x", "y"), ("y", "x"))

    def start_ring(unit, step, axis):
        return {
            (d, high): send(unit(step, axis, spot_on[axis], high), unit(step, axis, spot_on[axis], high), along[axis][d])
            for high in range(2)
            for d in range(2)
        }

    def forward_ring(copies, unit, step, axis):
        at = spot_on[axis]
        out = []
        for d in range(2):
            origin = wrap(at - 1) if d == 0 else wrap(at + 1)
            copies[d, d].wait_recv()
            out.append(send(unit(step, axis, origin, d), unit(step, axis, origin, d), along[axis][d]))
        return out

    lines, line_forwards = {}, {}
    for s in range(2):
        for copy in rest[s]:
            copy.wait_recv()
        own[s].wait()
        lines[s] = start_ring(line, s, order[s][0])
    for s in range(2):
        line_forwards[s] = forward_ring(lines[s], line, s, order[s][0])
    sheets, sheet_forwards, shared = {}, {}, []
    for s in range(2):
        lines[s][0, 1].wait_recv()
        lines[s][1, 0].wait_recv()
        for copy in line_forwards[s]:
            copy.wait_recv()
        sheets[s] = start_ring(sheet, s, order[s][1])

    def share(step, offset, high):
        axis = order[step][1]
        part = sheet(step, axis, wrap(spot_on[axis] + offset), high)
        shared.append(send(part, part, sibling))

    for s in range(2):
        for high in range(2):
            share(s, 0, high)
    for s in range(2):
        sheet_forwards[s] = forward_ring(sheets[s], sheet, s, order[s][1])
        share(s, -1, 0)
        share(s, 1, 1)
    for s in range(2):
        sheets[s][0, 1].wait_recv()
        share(s, -1, 1)
        sheets[s][1, 0].wait_recv()
        share(s, 1, 0)
    for s in range(2):
        for d in range(2):
            sheet_forwards[s][d].wait_recv()
            share(s, 2, d)
    for copy in shared:
        copy.wait_recv()
    for copy in send.copies:
        copy.wait_send()


def gather_tokens(tokens):
    steps, rows, quarter = tokens.shape
    out = pl.pallas_call(
        gather_kernel,
        out_shape=jax.ShapeDtypeStruct((steps, 2, RING, RING, rows, 4 * quarter), tokens.dtype),
        in_specs=[pl.BlockSpec(memory_space=pl.ANY)],
        out_specs=pl.BlockSpec(memory_space=pl.ANY),
        scratch_shapes=[
            pltpu.SemaphoreType.DMA((2,)),
            pltpu.SemaphoreType.DMA((GATHER_COPIES,)),
            pltpu.SemaphoreType.DMA((GATHER_COPIES,)),
        ],
        compiler_params=pltpu.CompilerParams(collective_id=0, has_side_effects=True),
        name="gather_tokens",
    )(tokens)
    return out.reshape(steps * 2 * RING * RING * rows, 4 * quarter)


REDUCE_COPIES = 2 * (2 + 4 + 2 + 2) + 2


def reduce_kernel(c_ref, out_ref, hop0, got0, sum0, hop1, got1, sum1, last, send_sem, recv_sem):
    z_hi, core, z_lo, y, x = place()
    along_z, along_x, along_y, _ = neighbours(z_hi, core, z_lo, y, x)
    partner = device(z_hi, core, 1 - z_lo, y, x)
    greet(along_x + along_y + [partner])
    along = {"x": along_x, "y": along_y}
    spot_on = {"x": x, "y": y}
    order = (("y", "x"), ("x", "y"))
    send = Sends(send_sem, recv_sem)

    def block(step, at):
        if order[step][0] == "y":
            return c_ref.at[step, :, at]
        return c_ref.at[step, :, :, at]

    hops, fulls = {}, {}
    for s in range(2):
        axis = order[s][0]
        at = spot_on[axis]
        hops[s] = [send(block(s, wrap(at + 2)).at[d], hop0.at[s, d], along[axis][d]) for d in range(2)]
    for s in range(2):
        axis = order[s][0]
        at = spot_on[axis]
        for d in range(2):
            target = wrap(at + 1) if d == 0 else wrap(at - 1)
            fulls[s, d] = [send(block(s, target).at[1 - d], got0.at[s, d, 1 - d], along[axis][d])]
    for s in range(2):
        axis = order[s][0]
        at = spot_on[axis]
        for d in range(2):
            target = wrap(at + 1) if d == 0 else wrap(at - 1)
            hops[s][d].wait_recv()
            mine = block(s, target)

            @pl.loop(0, RING)
            def _(i, mine=mine, s=s, d=d):
                total = mine[d, i].astype(jnp.float32) + hop0[s, d, i].astype(jnp.float32)
                hop0[s, d, i] = total.astype(jnp.bfloat16)

            fulls[s, d].append(send(hop0.at[s, d], got0.at[s, d, d], along[axis][d]))
    hops1, fulls1 = {}, {}
    for s in range(2):
        at = spot_on[order[s][0]]
        mine = block(s, at)
        for d in range(2):
            for copy in fulls[s, d]:
                copy.wait_recv()

        @pl.loop(0, RING)
        def _(i, mine=mine, s=s):
            for half in range(2):
                total = mine[half, i].astype(jnp.float32)
                total = total + got0[s, 0, half, i].astype(jnp.float32)
                total = total + got0[s, 1, half, i].astype(jnp.float32)
                sum0[s, half, i] = total.astype(jnp.bfloat16)

        axis = order[s][1]
        at = spot_on[axis]
        hops1[s] = [send(sum0.at[s, d, wrap(at + 2)], hop1.at[s, d], along[axis][d]) for d in range(2)]
    for s in range(2):
        axis = order[s][1]
        at = spot_on[axis]
        for d in range(2):
            target = wrap(at + 1) if d == 0 else wrap(at - 1)
            hops1[s][d].wait_recv()
            total = sum0[s, d, target].astype(jnp.float32) + hop1[s, d].astype(jnp.float32)
            sum0[s, d, target] = total.astype(jnp.bfloat16)
            fulls1[s, d] = send(sum0.at[s, :, target], got1.at[s, d], along[axis][d])
    finals = []
    for s in range(2):
        at = spot_on[order[s][1]]
        for d in range(2):
            fulls1[s, d].wait_recv()
        for half in range(2):
            total = sum0[s, half, at].astype(jnp.float32)
            total = total + got1[s, 0, half].astype(jnp.float32)
            total = total + got1[s, 1, half].astype(jnp.float32)
            sum1[s, half] = total.astype(jnp.bfloat16)
        finals.append(send(sum1.at[s, 1 - z_lo], last.at[s], partner))
    for s in range(2):
        finals[s].wait_recv()
        total = sum1[s, z_lo].astype(jnp.float32) + last[s].astype(jnp.float32)
        out_ref[s] = total.astype(jnp.bfloat16)
    for copy in send.copies:
        copy.wait_send()


def reduce_outputs(parts):
    steps, _, _, _, rows, width = parts.shape
    dt = parts.dtype
    return pl.pallas_call(
        reduce_kernel,
        out_shape=jax.ShapeDtypeStruct((steps, rows, width), dt),
        in_specs=[pl.BlockSpec(memory_space=pltpu.VMEM)],
        out_specs=pl.BlockSpec(memory_space=pltpu.VMEM),
        scratch_shapes=[
            pltpu.VMEM((steps, 2, RING, rows, width), dt),
            pltpu.VMEM((steps, 2, 2, RING, rows, width), dt),
            pltpu.VMEM((steps, 2, RING, rows, width), dt),
            pltpu.VMEM((steps, 2, rows, width), dt),
            pltpu.VMEM((steps, 2, 2, rows, width), dt),
            pltpu.VMEM((steps, 2, rows, width), dt),
            pltpu.VMEM((steps, rows, width), dt),
            pltpu.SemaphoreType.DMA((REDUCE_COPIES,)),
            pltpu.SemaphoreType.DMA((REDUCE_COPIES,)),
        ],
        compiler_params=pltpu.CompilerParams(
            collective_id=1, has_side_effects=True, vmem_limit_bytes=40 * 1024 * 1024
        ),
        name="reduce_outputs",
    )(parts)


def from_partner(value, axis, bit):
    mask = 2**bit
    pairs = [(source, source ^ mask) for source in range(lax.axis_size(axis))]
    return lax.ppermute(value, axis, pairs)


def per_device(tokens, logits, routes, held, swapped, w_gate, w_up, w_down):
    exp_count = lax.axis_size("exp")
    own_index = lax.axis_index("exp")
    half_count = exp_count // 2
    steps, rows_here, quarter = tokens.shape
    others = [from_partner(w, "exp", exp_count.bit_length() - 2) for w in (w_gate, w_up, w_down)]
    own_flag = swapped[own_index % half_count]

    score = jax.nn.sigmoid(logits)
    weight = score / jnp.sum(score, axis=-1, keepdims=True)
    expert_ids = jnp.arange(exp_count, dtype=jnp.int32)
    named = routes[:, :, :, None] == expert_ids
    table = jnp.sum(jnp.where(named, weight[:, :, :, None], 0.0), axis=2)
    everyone = lax.all_gather(table, "exp", axis=1, tiled=True)
    own_expert = held[own_index]
    own_weight = jnp.sum(jnp.where(expert_ids == own_expert, everyone, 0.0), axis=2)

    rows = gather_tokens(tokens)
    gate_tile, up_tile, down_tile = w_gate[0], w_up[0], w_down[0]
    gate = jnp.dot(rows, gate_tile, preferred_element_type=jnp.float32)
    upper = jnp.dot(rows, up_tile, preferred_element_type=jnp.float32)
    hidden = (jax.nn.silu(gate) * upper).astype(jnp.bfloat16)
    hidden = lax.all_gather(hidden, "attn", axis=1, tiled=True)
    produced = jnp.dot(hidden, down_tile, preferred_element_type=jnp.float32).astype(jnp.bfloat16)
    scaled = (2.5 * own_weight.reshape(-1)[:, None] * produced.astype(jnp.float32)).astype(jnp.bfloat16)
    mixed = reduce_outputs(scaled.reshape(steps, 2, RING, RING, rows_here, quarter))

    own_flag, mixed = lax.optimization_barrier((own_flag, mixed))
    afters = [jnp.where(own_flag == 1, other, w) for other, w in zip(others, (w_gate, w_up, w_down))]
    return (mixed, *afters)


def solution(mesh):
    in_specs = (
        P(None, "exp", "attn"),
        P(None, "exp", None),
        P(None, "exp", None),
        P(),
        P(),
        P("exp", None, "attn"),
        P("exp", None, "attn"),
        P("exp", None, "attn"),
    )
    out_specs = (
        P(None, "exp", "attn"),
        P("exp", None, "attn"),
        P("exp", None, "attn"),
        P("exp", None, "attn"),
    )
    return jax.shard_map(
        per_device, mesh=mesh, in_specs=in_specs, out_specs=out_specs, check_vma=False
    )
```

```python
import jax
import jax.numpy as jnp
from jax import lax
from jax.experimental import pallas as pl
from jax.experimental.pallas import tpu as pltpu
from jax.sharding import PartitionSpec as P

RING = 4


def wrap(value):
    return lax.rem(value + RING, RING)


def place():
    attn = lax.axis_index("attn")
    exp = lax.axis_index("exp")
    z_hi, core = attn // 2, lax.rem(attn, 2)
    z_lo, y, x = exp // 16, lax.rem(exp // 4, 4), lax.rem(exp, 4)
    return z_hi, core, z_lo, y, x


def device(z_hi, core, z_lo, y, x):
    return {"attn": z_hi * 2 + core, "exp": z_lo * 16 + y * 4 + x}


def neighbours(z_hi, core, z_lo, y, x):
    z = z_hi * 2 + z_lo
    right_z, left_z = wrap(z + 1), wrap(z - 1)
    along_z = [device(n // 2, core, lax.rem(n, 2), y, x) for n in (right_z, left_z)]
    along_x = [device(z_hi, core, z_lo, y, n) for n in (wrap(x + 1), wrap(x - 1))]
    along_y = [device(z_hi, core, z_lo, n, x) for n in (wrap(y + 1), wrap(y - 1))]
    return along_z, along_x, along_y, device(z_hi, 1 - core, z_lo, y, x)


def greet(devices):
    barrier = pltpu.get_barrier_semaphore()
    for other in devices:
        pl.semaphore_signal(barrier, inc=1, device_id=other, device_id_type=pl.DeviceIdType.MESH)
    pl.semaphore_wait(barrier, len(devices))


class Sends:
    def __init__(self, send_sem, recv_sem):
        self.send_sem, self.recv_sem, self.copies = send_sem, recv_sem, []

    def __call__(self, src, dst, to):
        k = len(self.copies)
        copy = pltpu.make_async_remote_copy(
            src_ref=src,
            dst_ref=dst,
            send_sem=self.send_sem.at[k],
            recv_sem=self.recv_sem.at[k],
            device_id=to,
            device_id_type=pl.DeviceIdType.MESH,
        )
        copy.start()
        self.copies.append(copy)
        return copy


STEPS = 2
PIECES = 16
EARLY, LATE = 20, 42
COPIES = 6 + 12 + 12 + 16 + 8 + 2 * (2 + 4 + 2 + 2) + 2
TILES = 8
EXTRA = 128


def layer_kernel(
    tok_ref, pick_ref, wg_ref, wu_ref, wd_ref,
    mixed_ref, og_ref, ou_ref, od_ref, all_ref,
    wg_v, wu_v, wd_v, tile_v, hall, relay, sel_v, wcol_v, c_v,
    hop0, got0, sum0, hop1, got1, sum1, last,
    local_sem, tile_sem, send_sem, recv_sem, swap_send, swap_recv,
):
    z_hi, core, z_lo, y, x = place()
    along_z, along_x, along_y, sibling = neighbours(z_hi, core, z_lo, y, x)
    partner = device(z_hi, core, 1 - z_lo, y, x)
    z = z_hi * 2 + z_lo
    attn = z_hi * 2 + core
    wide = tok_ref.shape[2]
    quarter = wide - EXTRA
    part = wg_ref.shape[1]
    send = Sends(send_sem, recv_sem)

    loads = [
        pltpu.make_async_copy(src, dst, local_sem.at[2 + k])
        for k, (src, dst) in enumerate(((wg_ref, wg_v), (wu_ref, wu_v), (wd_ref, wd_v)))
    ]
    for copy in loads:
        copy.start()
    greet(along_z + along_x + along_y + [sibling])

    swaps = []
    for src, dst in ((wg_ref, og_ref), (wu_ref, ou_ref), (wd_ref, od_ref)):
        size = src.shape[0] // PIECES
        for k in range(PIECES):
            n = len(swaps)
            swaps.append(
                pltpu.make_async_remote_copy(
                    src_ref=src.at[pl.ds(k * size, size)],
                    dst_ref=dst.at[pl.ds(k * size, size)],
                    send_sem=swap_send.at[n],
                    recv_sem=swap_recv.at[n],
                    device_id=partner,
                    device_id_type=pl.DeviceIdType.MESH,
                )
            )
    begun = [0]

    def swap_until(count):
        for copy in swaps[begun[0] : count]:
            copy.start()
        begun[0] = max(begun[0], count)

    def cols(high):
        return pl.ds(pl.multiple_of((high * 2 + core) * wide, 128), wide)

    def spot(step, at):
        return all_ref.at[step, lax.rem(at, 2), y, x, :, cols(at // 2)]

    own = [pltpu.make_async_copy(tok_ref.at[s], spot(s, z), local_sem.at[s]) for s in range(STEPS)]
    for copy in own:
        copy.start()
    first = {}
    for s in range(STEPS):
        for d in range(2):
            first[d, s] = send(tok_ref.at[s], spot(s, z), along_z[d])
    first[0, 0].wait_recv()
    forward0 = send(spot(0, wrap(z - 1)), spot(0, wrap(z - 1)), along_z[0])
    first[1, 1].wait_recv()
    forward1 = send(spot(1, wrap(z + 1)), spot(1, wrap(z + 1)), along_z[1])
    rest = {0: [first[1, 0], forward0], 1: [first[0, 1], forward1]}
    swap_until(EARLY)

    def line(step, axis, at, high):
        if axis == "x":
            return all_ref.at[step, :, y, at, :, cols(high)]
        return all_ref.at[step, :, at, x, :, cols(high)]

    def sheet(step, axis, at, high):
        if axis == "x":
            return all_ref.at[step, :, :, at, :, cols(high)]
        return all_ref.at[step, :, at, :, :, cols(high)]

    along = {"x": along_x, "y": along_y}
    spot_on = {"x": x, "y": y}
    order = (("x", "y"), ("y", "x"))

    def start_ring(unit, step, axis):
        at = spot_on[axis]
        return {
            (d, high): send(unit(step, axis, at, high), unit(step, axis, at, high), along[axis][d])
            for high in range(2)
            for d in range(2)
        }

    def forward_ring(copies, unit, step, axis):
        at = spot_on[axis]
        out = []
        for d in range(2):
            origin = wrap(at - 1) if d == 0 else wrap(at + 1)
            copies[d, d].wait_recv()
            out.append(send(unit(step, axis, origin, d), unit(step, axis, origin, d), along[axis][d]))
        return out

    lines, line_forwards = {}, {}
    for s in range(STEPS):
        for copy in rest[s]:
            copy.wait_recv()
        own[s].wait()
        lines[s] = start_ring(line, s, order[s][0])
    for s in range(STEPS):
        line_forwards[s] = forward_ring(lines[s], line, s, order[s][0])
    sheets, sheet_forwards, shared = {}, {}, []
    for s in range(STEPS):
        lines[s][0, 1].wait_recv()
        lines[s][1, 0].wait_recv()
        for copy in line_forwards[s]:
            copy.wait_recv()
        sheets[s] = start_ring(sheet, s, order[s][1])

    def share(step, offset, high):
        axis = order[step][1]
        unit = sheet(step, axis, wrap(spot_on[axis] + offset), high)
        shared.append(send(unit, unit, sibling))

    for s in range(STEPS):
        for high in range(2):
            share(s, 0, high)
    for s in range(STEPS):
        sheet_forwards[s] = forward_ring(sheets[s], sheet, s, order[s][1])
        share(s, -1, 0)
        share(s, 1, 1)
    for s in range(STEPS):
        sheets[s][0, 1].wait_recv()
        share(s, -1, 1)
        sheets[s][1, 0].wait_recv()
        share(s, 1, 0)
    for s in range(STEPS):
        for d in range(2):
            sheet_forwards[s][d].wait_recv()
            share(s, 2, d)
    for copy in shared:
        copy.wait_recv()
    for copy in loads:
        copy.wait()

    def tile_copy(t, slot):
        src = all_ref.at[t // 4, lax.rem(t // 2, 2), pl.ds(lax.rem(t, 2) * 2, 2)]
        return pltpu.make_async_copy(src, tile_v.at[slot], tile_sem.at[slot])

    span = tile_v.shape[1] * tile_v.shape[2] * tile_v.shape[3]
    slots = span // 2
    block = tile_v.shape[3]
    pick = pick_ref[...]

    tile_copy(0, 0).start()

    def gate_up(t, carry):
        slot = lax.rem(t, 2)
        tile_copy(t, slot).wait()

        @pl.when(t + 1 < TILES)
        def _():
            tile_copy(t + 1, 1 - slot).start()

        extra = tile_v[slot, :, :, :, quarter:wide].reshape(span, EXTRA)
        along_lanes = lax.dot_general(pick, extra, (((1,), (1,)), ((), ())), preferred_element_type=jnp.float32)
        mask = along_lanes > 0.0
        row_i = lax.broadcasted_iota(jnp.int32, (span, span), 0)
        col_i = lax.broadcasted_iota(jnp.int32, (span, span), 1)
        upto = jnp.where((row_i // block == col_i // block) & (row_i <= col_i), 1.0, 0.0).astype(jnp.bfloat16)
        count = jnp.dot(
            jnp.where(mask, 1.0, 0.0).astype(jnp.bfloat16), upto, preferred_element_type=jnp.float32
        )
        base = lax.broadcasted_iota(jnp.int32, count.shape, 1) // block * (block // 2) - 1
        where_to = jnp.where(mask, count + base.astype(jnp.float32), -1.0)[0:1, :]
        slot_i = lax.broadcasted_iota(jnp.int32, (slots, span), 0).astype(jnp.float32)
        sel = jnp.where(slot_i == where_to, 1.0, 0.0).astype(jnp.bfloat16)
        sel_v[t] = sel
        wcol = jnp.sum(extra.astype(jnp.float32) * pick[0:1].astype(jnp.float32), axis=1, keepdims=True)
        wcol_v[t] = jnp.broadcast_to(2.5 * wcol, (span, 128))
        gate = jnp.zeros((slots, part), jnp.float32)
        upper = jnp.zeros((slots, part), jnp.float32)
        for q in range(4):
            rows = tile_v[slot, :, :, :, q * wide : q * wide + quarter].reshape(span, quarter)
            served = jnp.dot(sel, rows, preferred_element_type=jnp.float32).astype(jnp.bfloat16)
            w = pl.ds(q * quarter, quarter)
            gate = gate + jnp.dot(served, wg_v[w, :], preferred_element_type=jnp.float32)
            upper = upper + jnp.dot(served, wu_v[w, :], preferred_element_type=jnp.float32)
        act = gate / (1.0 + jnp.exp(-gate)) * upper
        hall[attn, t] = act.astype(jnp.bfloat16)
        return carry

    lax.fori_loop(0, TILES, gate_up, 0)

    half = [pl.ds(0, TILES // 2), pl.ds(TILES // 2, TILES // 2)]
    hops = [send(hall.at[attn, half[d]], relay.at[d], along_z[d]) for d in range(2)]
    to_core = [send(hall.at[attn], hall.at[attn], sibling)]
    far = []
    for d in range(2):
        hops[d].wait_recv()
        origin = (wrap(z - 1) if d == 0 else wrap(z + 1)) // 2 * 2 + core
        far.append(send(relay.at[d], hall.at[origin, half[d]], along_z[d]))
    swap_until(LATE)
    opposite = (1 - z_hi) * 2 + core
    for d in range(2):
        far[d].wait_recv()
        to_core.append(send(hall.at[opposite, half[d]], hall.at[opposite, half[d]], sibling))
    for copy in to_core:
        copy.wait_recv()

    def down(t, carry):
        total = jnp.zeros((slots, quarter), jnp.float32)
        for a in range(4):
            total = total + jnp.dot(
                hall[a, t], wd_v[pl.ds(a * part, part), :], preferred_element_type=jnp.float32
            )
        produced = total.astype(jnp.bfloat16)
        spread = lax.dot_general(
            sel_v[t], produced, (((0,), (0,)), ((), ())), preferred_element_type=jnp.float32
        )
        scaled = (wcol_v[t][:, 0:1] * spread).astype(jnp.bfloat16)
        c_v[t // 4, lax.rem(t // 2, 2), pl.ds(lax.rem(t, 2) * 2, 2)] = scaled.reshape(c_v.shape[2] // 2, *c_v.shape[3:])
        return carry

    lax.fori_loop(0, TILES, down, 0)

    flow = (("y", "x"), ("x", "y"))

    def lane(step, at):
        if flow[step][0] == "y":
            return c_v.at[step, :, at]
        return c_v.at[step, :, :, at]

    hops, fulls = {}, {}
    for s in range(STEPS):
        axis = flow[s][0]
        at = spot_on[axis]
        hops[s] = [send(lane(s, wrap(at + 2)).at[d], hop0.at[s, d], along[axis][d]) for d in range(2)]
    for s in range(STEPS):
        axis = flow[s][0]
        at = spot_on[axis]
        for d in range(2):
            target = wrap(at + 1) if d == 0 else wrap(at - 1)
            fulls[s, d] = [send(lane(s, target).at[1 - d], got0.at[s, d, 1 - d], along[axis][d])]
    for s in range(STEPS):
        axis = flow[s][0]
        at = spot_on[axis]
        for d in range(2):
            target = wrap(at + 1) if d == 0 else wrap(at - 1)
            hops[s][d].wait_recv()
            mine = lane(s, target)

            @pl.loop(0, RING)
            def _(i, mine=mine, s=s, d=d):
                total = mine[d, i].astype(jnp.float32) + hop0[s, d, i].astype(jnp.float32)
                hop0[s, d, i] = total.astype(jnp.bfloat16)

            fulls[s, d].append(send(hop0.at[s, d], got0.at[s, d, d], along[axis][d]))
    hops1, fulls1 = {}, {}
    for s in range(STEPS):
        at = spot_on[flow[s][0]]
        mine = lane(s, at)
        for d in range(2):
            for copy in fulls[s, d]:
                copy.wait_recv()

        @pl.loop(0, RING)
        def _(i, mine=mine, s=s):
            for h in range(2):
                total = mine[h, i].astype(jnp.float32)
                total = total + got0[s, 0, h, i].astype(jnp.float32)
                total = total + got0[s, 1, h, i].astype(jnp.float32)
                sum0[s, h, i] = total

        axis = flow[s][1]
        at = spot_on[axis]
        hops1[s] = [send(sum0.at[s, d, wrap(at + 2)], hop1.at[s, d], along[axis][d]) for d in range(2)]
    for s in range(STEPS):
        axis = flow[s][1]
        at = spot_on[axis]
        for d in range(2):
            target = wrap(at + 1) if d == 0 else wrap(at - 1)
            hops1[s][d].wait_recv()
            sum0[s, d, target] = sum0[s, d, target] + hop1[s, d]
            fulls1[s, d] = send(sum0.at[s, :, target], got1.at[s, d], along[axis][d])
    finals = []
    for s in range(STEPS):
        at = spot_on[flow[s][1]]
        for d in range(2):
            fulls1[s, d].wait_recv()
        away = 1 - z_lo
        sum1[s] = (sum0[s, away, at] + got1[s, 0, away] + got1[s, 1, away]).astype(jnp.bfloat16)
        finals.append(send(sum1.at[s], last.at[s], partner))
    swap_until(3 * PIECES)
    for s in range(STEPS):
        at = spot_on[flow[s][1]]
        finals[s].wait_recv()
        total = sum0[s, z_lo, at] + got1[s, 0, z_lo] + got1[s, 1, z_lo] + last[s].astype(jnp.float32)
        mixed_ref[s] = total.astype(jnp.bfloat16)
    for copy in send.copies:
        copy.wait_send()
    for copy in swaps:
        copy.wait()


def layer(tokens, pick, w_gate, w_up, w_down):
    steps, rows, wide = tokens.shape
    quarter = wide - EXTRA
    dt = tokens.dtype
    part = w_gate.shape[1]
    plane = (2, RING, RING, rows)
    hbm = pl.BlockSpec(memory_space=pl.ANY)
    vmem = pl.BlockSpec(memory_space=pltpu.VMEM)
    like = lambda a: jax.ShapeDtypeStruct(a.shape, a.dtype)
    return pl.pallas_call(
        layer_kernel,
        out_shape=(
            jax.ShapeDtypeStruct((steps, rows, quarter), dt),
            like(w_gate),
            like(w_up),
            like(w_down),
            jax.ShapeDtypeStruct((steps, *plane, 4 * wide), dt),
        ),
        in_specs=[hbm, vmem, hbm, hbm, hbm],
        out_specs=(vmem, hbm, hbm, hbm, hbm),
        scratch_shapes=[
            pltpu.VMEM(w_gate.shape, dt),
            pltpu.VMEM(w_up.shape, dt),
            pltpu.VMEM(w_down.shape, dt),
            pltpu.VMEM((2, 2, RING, rows, 4 * wide), dt),
            pltpu.VMEM((4, TILES, 4 * rows, part), dt),
            pltpu.VMEM((2, TILES // 2, 4 * rows, part), dt),
            pltpu.VMEM((TILES, 4 * rows, 8 * rows), dt),
            pltpu.VMEM((TILES, 8 * rows, 128), jnp.float32),
            pltpu.VMEM((steps, *plane, quarter), dt),
            pltpu.VMEM((steps, 2, RING, rows, quarter), dt),
            pltpu.VMEM((steps, 2, 2, RING, rows, quarter), dt),
            pltpu.VMEM((steps, 2, RING, rows, quarter), jnp.float32),
            pltpu.VMEM((steps, 2, rows, quarter), jnp.float32),
            pltpu.VMEM((steps, 2, 2, rows, quarter), jnp.float32),
            pltpu.VMEM((steps, rows, quarter), dt),
            pltpu.VMEM((steps, rows, quarter), dt),
            pltpu.SemaphoreType.DMA((5,)),
            pltpu.SemaphoreType.DMA((2,)),
            pltpu.SemaphoreType.DMA((COPIES,)),
            pltpu.SemaphoreType.DMA((COPIES,)),
            pltpu.SemaphoreType.DMA((3 * PIECES,)),
            pltpu.SemaphoreType.DMA((3 * PIECES,)),
        ],
        compiler_params=pltpu.CompilerParams(
            collective_id=0, has_side_effects=True, vmem_limit_bytes=58 * 1024 * 1024
        ),
        name="layer",
    )(tokens, pick, w_gate, w_up, w_down)[:4]


def three_parts(value):
    parts = []
    for _ in range(3):
        part = lax.reduce_precision(value, exponent_bits=8, mantissa_bits=7)
        parts.append(part.astype(jnp.bfloat16))
        value = value - part
    return parts


def per_device(tokens, logits, routes, held, swapped, w_gate, w_up, w_down):
    exp_count = lax.axis_size("exp")
    own_index = lax.axis_index("exp")
    own_flag = swapped[own_index % (exp_count // 2)]

    score = jax.nn.sigmoid(logits)
    weight = score / jnp.sum(score, axis=-1, keepdims=True)
    expert_ids = jnp.arange(exp_count, dtype=jnp.int32)
    named = routes[:, :, :, None] == expert_ids
    table = jnp.sum(jnp.where(named, weight[:, :, :, None], 0.0), axis=2)
    parts = three_parts(table)
    beside = jnp.concatenate([tokens, *parts, jnp.zeros_like(parts[0])], axis=2)
    lanes = jnp.arange(EXTRA, dtype=jnp.int32)
    own_expert = held[own_index]
    picked = (lanes % exp_count == own_expert) & (lanes < 3 * exp_count)
    pick = jnp.broadcast_to(picked.astype(jnp.bfloat16)[None, :], (16, EXTRA))

    mixed, *others = layer(beside, pick, w_gate[0], w_up[0], w_down[0])
    afters = [
        jnp.where(own_flag == 1, other[None], w) for other, w in zip(others, (w_gate, w_up, w_down))
    ]
    return (mixed, *afters)


def solution(mesh):
    in_specs = (
        P(None, "exp", "attn"),
        P(None, "exp", None),
        P(None, "exp", None),
        P(),
        P(),
        P("exp", None, "attn"),
        P("exp", None, "attn"),
        P("exp", None, "attn"),
    )
    out_specs = (
        P(None, "exp", "attn"),
        P("exp", None, "attn"),
        P("exp", None, "attn"),
        P("exp", None, "attn"),
    )
    return jax.shard_map(
        per_device, mesh=mesh, in_specs=in_specs, out_specs=out_specs, check_vma=False
    )
```

```python
import functools

import jax
import jax.numpy as jnp
from jax import lax
from jax.experimental import pallas as pl
from jax.experimental.pallas import tpu as pltpu
from jax.sharding import PartitionSpec as P

RING = 4


def wrap(value):
    return lax.rem(value + RING, RING)


def place():
    attn = lax.axis_index("attn")
    exp = lax.axis_index("exp")
    z_hi, core = attn // 2, lax.rem(attn, 2)
    z_lo, y, x = exp // 16, lax.rem(exp // 4, 4), lax.rem(exp, 4)
    return z_hi, core, z_lo, y, x


def device(z_hi, core, z_lo, y, x):
    return {"attn": z_hi * 2 + core, "exp": z_lo * 16 + y * 4 + x}


def neighbours(z_hi, core, z_lo, y, x):
    z = z_hi * 2 + z_lo
    right_z, left_z = wrap(z + 1), wrap(z - 1)
    along_z = [device(n // 2, core, lax.rem(n, 2), y, x) for n in (right_z, left_z)]
    along_x = [device(z_hi, core, z_lo, y, n) for n in (wrap(x + 1), wrap(x - 1))]
    along_y = [device(z_hi, core, z_lo, n, x) for n in (wrap(y + 1), wrap(y - 1))]
    return along_z, along_x, along_y, device(z_hi, 1 - core, z_lo, y, x)


def greet(devices):
    barrier = pltpu.get_barrier_semaphore()
    for other in devices:
        pl.semaphore_signal(barrier, inc=1, device_id=other, device_id_type=pl.DeviceIdType.MESH)
    pl.semaphore_wait(barrier, len(devices))


class Sends:
    def __init__(self, send_sem, recv_sem):
        self.send_sem, self.recv_sem, self.copies = send_sem, recv_sem, []

    def __call__(self, src, dst, to):
        k = len(self.copies)
        copy = pltpu.make_async_remote_copy(
            src_ref=src,
            dst_ref=dst,
            send_sem=self.send_sem.at[k],
            recv_sem=self.recv_sem.at[k],
            device_id=to,
            device_id_type=pl.DeviceIdType.MESH,
        )
        copy.start()
        self.copies.append(copy)
        return copy


STEPS = 2
PIECES = 16
SLAB = 64
EARLY, LATE = 26, 41
COPIES = 6 + 12 + 12 + 16 + 8 + 2 * (2 + 4 + 2 + 2) + 2
TILES = 8
EXTRA = 128


def layer_kernel(
    held_ref, swapped_ref, tokens_ref, logits_ref, routes_ref, wg_ref, wu_ref, wd_ref,
    mixed_ref, og_ref, ou_ref, od_ref, all_ref,
    wg_v, wu_v, wd_v, tok_ref, tile_v, hall, relay, sel_v, wcol_v,
    hop0, got0, sum0, hop1, got1, sum1, last,
    local_sem, tile_sem, send_sem, recv_sem, swap_send, swap_recv,
):
    z_hi, core, z_lo, y, x = place()
    along_z, along_x, along_y, sibling = neighbours(z_hi, core, z_lo, y, x)
    partner = device(z_hi, core, 1 - z_lo, y, x)
    z = z_hi * 2 + z_lo
    attn = z_hi * 2 + core
    wide = tok_ref.shape[2]
    quarter = wide - EXTRA
    part = wg_ref.shape[1]
    send = Sends(send_sem, recv_sem)

    loads = [
        pltpu.make_async_copy(src, dst, local_sem.at[2 + k])
        for k, (src, dst) in enumerate(((wg_ref, wg_v), (wu_ref, wu_v), (wd_ref, wd_v)))
    ]
    tok_load = pltpu.make_async_copy(tokens_ref, tok_ref.at[:, :, pl.ds(0, quarter)], local_sem.at[5])
    for copy in [tok_load, *loads]:
        copy.start()
    greet(along_z + along_x + along_y + [sibling])

    swaps = []
    for src, dst in ((wg_ref, og_ref), (wu_ref, ou_ref), (wd_ref, od_ref)):
        size = src.shape[0] // PIECES
        for k in range(PIECES):
            n = len(swaps)
            swaps.append(
                pltpu.make_async_remote_copy(
                    src_ref=src.at[pl.ds(k * size, size)],
                    dst_ref=dst.at[pl.ds(k * size, size)],
                    send_sem=swap_send.at[n],
                    recv_sem=swap_recv.at[n],
                    device_id=partner,
                    device_id_type=pl.DeviceIdType.MESH,
                )
            )
    begun = [0]

    def swap_until(count):
        for copy in swaps[begun[0] : count]:
            copy.start()
        begun[0] = max(begun[0], count)

    def cols(high):
        return pl.ds(pl.multiple_of((high * 2 + core) * wide, 128), wide)

    def spot(step, at):
        return all_ref.at[step, lax.rem(at, 2), y, x, :, cols(at // 2)]

    exp_count = held_ref.shape[0]
    lane_i = lax.broadcasted_iota(jnp.int32, (logits_ref.shape[1], EXTRA), 1)
    expert_i = lax.rem(lane_i, exp_count)
    for s in range(STEPS):
        score = 1.0 / (1.0 + jnp.exp(-logits_ref[s]))
        weight = score / jnp.sum(score, axis=1, keepdims=True)
        names = routes_ref[s]
        table = jnp.zeros(lane_i.shape, jnp.float32)
        for k in range(names.shape[1]):
            table = table + jnp.where(names[:, k : k + 1] == expert_i, weight[:, k : k + 1], 0.0)
        high = table.astype(jnp.bfloat16).astype(jnp.float32)
        middle = (table - high).astype(jnp.bfloat16).astype(jnp.float32)
        low = table - high - middle
        parts = jnp.where(lane_i < exp_count, high, jnp.where(lane_i < 2 * exp_count, middle, low))
        parts = jnp.where(lane_i < 3 * exp_count, parts, 0.0)
        tok_ref[s, :, quarter:wide] = parts.astype(jnp.bfloat16)
    tok_load.wait()

    own = [pltpu.make_async_copy(tok_ref.at[s], spot(s, z), local_sem.at[s]) for s in range(STEPS)]
    for copy in own:
        copy.start()
    beyond = wrap(z + 2 * z_lo - 1)
    beyond_device = device(beyond // 2, core, lax.rem(beyond, 2), y, x)
    near = [send(tok_ref.at[s], spot(s, z), partner) for s in range(STEPS)]
    swap_until(EARLY)
    rest = {s: [send(tok_ref.at[s], spot(s, z), beyond_device)] for s in range(STEPS)}
    pair = z + 1 - 2 * z_lo
    for s in range(STEPS):
        near[s].wait_recv()
        rest[s].append(send(spot(s, pair), spot(s, pair), beyond_device))

    def line(step, axis, at, high):
        if axis == "x":
            return all_ref.at[step, :, y, at, :, cols(high)]
        return all_ref.at[step, :, at, x, :, cols(high)]

    def sheet(step, axis, at, high):
        if axis == "x":
            return all_ref.at[step, :, :, at, :, cols(high)]
        return all_ref.at[step, :, at, :, :, cols(high)]

    along = {"x": along_x, "y": along_y}
    spot_on = {"x": x, "y": y}
    order = (("x", "y"), ("y", "x"))

    def start_ring(unit, step, axis):
        at = spot_on[axis]
        return {
            (d, high): send(unit(step, axis, at, high), unit(step, axis, at, high), along[axis][d])
            for high in range(2)
            for d in range(2)
        }

    def forward_ring(copies, unit, step, axis):
        at = spot_on[axis]
        out = []
        for d in range(2):
            origin = wrap(at - 1) if d == 0 else wrap(at + 1)
            copies[d, d].wait_recv()
            out.append(send(unit(step, axis, origin, d), unit(step, axis, origin, d), along[axis][d]))
        return out

    lines, line_forwards = {}, {}
    for s in range(STEPS):
        for copy in rest[s]:
            copy.wait_recv()
        own[s].wait()
        lines[s] = start_ring(line, s, order[s][0])
    for s in range(STEPS):
        line_forwards[s] = forward_ring(lines[s], line, s, order[s][0])
    sheets, sheet_forwards, shared = {}, {}, []
    for s in range(STEPS):
        lines[s][0, 1].wait_recv()
        lines[s][1, 0].wait_recv()
        for copy in line_forwards[s]:
            copy.wait_recv()
        sheets[s] = start_ring(sheet, s, order[s][1])

    def share(step, offset, high):
        axis = order[step][1]
        unit = sheet(step, axis, wrap(spot_on[axis] + offset), high)
        shared.append(send(unit, unit, sibling))

    for s in range(STEPS):
        for high in range(2):
            share(s, 0, high)
    for s in range(STEPS):
        sheet_forwards[s] = forward_ring(sheets[s], sheet, s, order[s][1])
        share(s, -1, 0)
        share(s, 1, 1)
    for s in range(STEPS):
        sheets[s][0, 1].wait_recv()
        share(s, -1, 1)
        sheets[s][1, 0].wait_recv()
        share(s, 1, 0)
    for s in range(STEPS):
        for d in range(2):
            sheet_forwards[s][d].wait_recv()
            share(s, 2, d)
    for copy in shared:
        copy.wait_recv()
    for copy in loads:
        copy.wait()

    def tile_copy(t, slot):
        src = all_ref.at[t // 4, lax.rem(t // 2, 2), pl.ds(lax.rem(t, 2) * 2, 2)]
        return pltpu.make_async_copy(src, tile_v.at[slot], tile_sem.at[slot])

    span = tile_v.shape[1] * tile_v.shape[2] * tile_v.shape[3]
    slots = span // 2
    block = tile_v.shape[3]
    own_expert = held_ref[lax.axis_index("exp")]
    pick_i = lax.broadcasted_iota(jnp.int32, (16, EXTRA), 1)
    pick = jnp.where(
        (lax.rem(pick_i, exp_count) == own_expert) & (pick_i < 3 * exp_count), 1.0, 0.0
    ).astype(jnp.bfloat16)

    tile_copy(0, 0).start()

    def gate_up(t, carry):
        slot = lax.rem(t, 2)
        tile_copy(t, slot).wait()

        @pl.when(t + 1 < TILES)
        def _():
            tile_copy(t + 1, 1 - slot).start()

        extra = tile_v[slot, :, :, :, quarter:wide].reshape(span, EXTRA)
        along_lanes = lax.dot_general(pick, extra, (((1,), (1,)), ((), ())), preferred_element_type=jnp.float32)
        mask = along_lanes > 0.0
        row_i = lax.broadcasted_iota(jnp.int32, (span, span), 0)
        col_i = lax.broadcasted_iota(jnp.int32, (span, span), 1)
        upto = jnp.where((row_i // block == col_i // block) & (row_i <= col_i), 1.0, 0.0).astype(jnp.bfloat16)
        count = jnp.dot(
            jnp.where(mask, 1.0, 0.0).astype(jnp.bfloat16), upto, preferred_element_type=jnp.float32
        )
        base = lax.broadcasted_iota(jnp.int32, count.shape, 1) // block * (block // 2) - 1
        where_to = jnp.where(mask, count + base.astype(jnp.float32), -1.0)[0:1, :]
        slot_i = lax.broadcasted_iota(jnp.int32, (slots, span), 0).astype(jnp.float32)
        sel = jnp.where(slot_i == where_to, 1.0, 0.0).astype(jnp.bfloat16)
        sel_v[t] = sel
        wcol = jnp.sum(extra.astype(jnp.float32) * pick[0:1].astype(jnp.float32), axis=1, keepdims=True)
        wcol_v[t] = jnp.broadcast_to(2.5 * wcol, (span, 128))
        gate = jnp.zeros((slots, part), jnp.float32)
        upper = jnp.zeros((slots, part), jnp.float32)
        for q in range(4):
            rows = tile_v[slot, :, :, :, q * wide : q * wide + quarter].reshape(span, quarter)
            served = jnp.dot(sel, rows, preferred_element_type=jnp.float32).astype(jnp.bfloat16)
            w = pl.ds(q * quarter, quarter)
            gate = gate + jnp.dot(served, wg_v[w, :], preferred_element_type=jnp.float32)
            upper = upper + jnp.dot(served, wu_v[w, :], preferred_element_type=jnp.float32)
        act = gate / (1.0 + jnp.exp(-gate)) * upper
        hall[attn, t] = act.astype(jnp.bfloat16)
        return carry

    lax.fori_loop(0, TILES, gate_up, 0)

    half = [pl.ds(0, TILES // 2), pl.ds(TILES // 2, TILES // 2)]
    hops = [send(hall.at[attn, half[d]], relay.at[d], along_z[d]) for d in range(2)]
    to_core = [send(hall.at[attn], hall.at[attn], sibling)]
    far = []
    for d in range(2):
        hops[d].wait_recv()
        origin = (wrap(z - 1) if d == 0 else wrap(z + 1)) // 2 * 2 + core
        far.append(send(relay.at[d], hall.at[origin, half[d]], along_z[d]))
    swap_until(LATE)
    opposite = (1 - z_hi) * 2 + core
    for d in range(2):
        far[d].wait_recv()
        to_core.append(send(hall.at[opposite, half[d]], hall.at[opposite, half[d]], sibling))
    for copy in to_core:
        copy.wait_recv()

    def down(step, t, carry):
        total = jnp.zeros((slots, quarter), jnp.float32)
        for a in range(4):
            total = total + jnp.dot(
                hall[a, t], wd_v[pl.ds(a * part, part), :], preferred_element_type=jnp.float32
            )
        produced = total.astype(jnp.bfloat16)
        spread = lax.dot_general(
            sel_v[t], produced, (((0,), (0,)), ((), ())), preferred_element_type=jnp.float32
        )
        scaled = (wcol_v[t][:, 0:1] * spread).astype(jnp.bfloat16)
        scaled = scaled.reshape(2, RING, block, quarter)
        low = lax.rem(t // 2, 2)
        for k in range(2):
            row = lax.rem(t, 2) * 2 + k
            if step == 0:
                tile_v[0, low, :, :, pl.ds(pl.multiple_of(row * quarter, 128), quarter)] = scaled[k]
            else:
                for i in range(RING):
                    tile_v[1, low, row, :, i * quarter : (i + 1) * quarter] = scaled[k, i]
        return carry

    for step in range(STEPS):
        lax.fori_loop(step * TILES // 2, (step + 1) * TILES // 2, functools.partial(down, step), 0)

    flow = (("y", "x"), ("x", "y"))

    def lane(step, at):
        return tile_v.at[step, :, :, :, pl.ds(pl.multiple_of(at * quarter, 128), quarter)]

    hops, fulls = {}, {}
    for s in range(STEPS):
        axis = flow[s][0]
        at = spot_on[axis]
        hops[s] = [send(lane(s, wrap(at + 2)).at[d], hop0.at[s, d], along[axis][d]) for d in range(2)]
    for s in range(STEPS):
        axis = flow[s][0]
        at = spot_on[axis]
        for d in range(2):
            target = wrap(at + 1) if d == 0 else wrap(at - 1)
            fulls[s, d] = [send(lane(s, target).at[1 - d], got0.at[s, d, 1 - d], along[axis][d])]
    for s in range(STEPS):
        axis = flow[s][0]
        at = spot_on[axis]
        for d in range(2):
            target = wrap(at + 1) if d == 0 else wrap(at - 1)
            hops[s][d].wait_recv()
            mine = lane(s, target)

            @pl.loop(0, RING)
            def _(i, mine=mine, s=s, d=d):
                total = mine[d, i].astype(jnp.float32) + hop0[s, d, i].astype(jnp.float32)
                hop0[s, d, i] = total.astype(jnp.bfloat16)

            fulls[s, d].append(send(hop0.at[s, d], got0.at[s, d, d], along[axis][d]))
    hops1, fulls1 = {}, {}
    for s in range(STEPS):
        at = spot_on[flow[s][0]]
        mine = lane(s, at)
        for d in range(2):
            for copy in fulls[s, d]:
                copy.wait_recv()

        @pl.loop(0, RING)
        def _(i, mine=mine, s=s):
            for h in range(2):
                total = mine[h, i].astype(jnp.float32)
                total = total + got0[s, 0, h, i].astype(jnp.float32)
                total = total + got0[s, 1, h, i].astype(jnp.float32)
                sum0[s, h, i] = total

        axis = flow[s][1]
        at = spot_on[axis]
        hops1[s] = [send(sum0.at[s, d, wrap(at + 2)], hop1.at[s, d], along[axis][d]) for d in range(2)]
    for s in range(STEPS):
        axis = flow[s][1]
        at = spot_on[axis]
        for d in range(2):
            target = wrap(at + 1) if d == 0 else wrap(at - 1)
            hops1[s][d].wait_recv()
            sum0[s, d, target] = sum0[s, d, target] + hop1[s, d]
            fulls1[s, d] = send(sum0.at[s, :, target], got1.at[s, d], along[axis][d])
    finals = []
    for s in range(STEPS):
        at = spot_on[flow[s][1]]
        for d in range(2):
            fulls1[s, d].wait_recv()
        away = 1 - z_lo
        sum1[s] = (sum0[s, away, at] + got1[s, 0, away] + got1[s, 1, away]).astype(jnp.bfloat16)
        finals.append(send(sum1.at[s], last.at[s], partner))
    swap_until(3 * PIECES)
    for s in range(STEPS):
        at = spot_on[flow[s][1]]
        finals[s].wait_recv()
        total = sum0[s, z_lo, at] + got1[s, 0, z_lo] + got1[s, 1, z_lo] + last[s].astype(jnp.float32)
        mixed_ref[s] = total.astype(jnp.bfloat16)
    flag = swapped_ref[lax.rem(lax.axis_index("exp"), swapped_ref.shape[0])]
    n = 0
    for dst, src in ((og_ref, wg_v), (ou_ref, wu_v), (od_ref, wd_v)):
        size = src.shape[0] // PIECES
        for k in range(PIECES):
            swaps[n].wait_recv()

            @pl.loop(0, size // SLAB)
            def _(i, dst=dst, src=src, k=k, size=size):
                at = pl.ds(pl.multiple_of(k * size + i * SLAB, SLAB), SLAB)
                trade = jnp.full((SLAB, src.shape[1]), flag, jnp.int32) == 1
                dst[at, :] = jnp.where(trade, dst[at, :], src[at, :])

            n += 1
    for copy in send.copies + swaps:
        copy.wait_send()


def layer(held, swapped, tokens, logits, routes, w_gate, w_up, w_down):
    steps, rows, quarter = tokens.shape
    wide = quarter + EXTRA
    dt = tokens.dtype
    part = w_gate.shape[1]
    plane = (2, RING, RING, rows)
    hbm = pl.BlockSpec(memory_space=pl.ANY)
    vmem = pl.BlockSpec(memory_space=pltpu.VMEM)
    smem = pl.BlockSpec(memory_space=pltpu.SMEM)
    like = lambda a: jax.ShapeDtypeStruct(a.shape, a.dtype)
    return pl.pallas_call(
        layer_kernel,
        out_shape=(
            jax.ShapeDtypeStruct((steps, rows, quarter), dt),
            like(w_gate),
            like(w_up),
            like(w_down),
            jax.ShapeDtypeStruct((steps, *plane, 4 * wide), dt),
        ),
        in_specs=[smem, smem, hbm, vmem, vmem, hbm, hbm, hbm],
        out_specs=(vmem, vmem, vmem, vmem, hbm),
        scratch_shapes=[
            pltpu.VMEM(w_gate.shape, dt),
            pltpu.VMEM(w_up.shape, dt),
            pltpu.VMEM(w_down.shape, dt),
            pltpu.VMEM((steps, rows, wide), dt),
            pltpu.VMEM((2, 2, RING, rows, 4 * wide), dt),
            pltpu.VMEM((4, TILES, 4 * rows, part), dt),
            pltpu.VMEM((2, TILES // 2, 4 * rows, part), dt),
            pltpu.VMEM((TILES, 4 * rows, 8 * rows), dt),
            pltpu.VMEM((TILES, 8 * rows, 128), jnp.float32),
            pltpu.VMEM((steps, 2, RING, rows, quarter), dt),
            pltpu.VMEM((steps, 2, 2, RING, rows, quarter), dt),
            pltpu.VMEM((steps, 2, RING, rows, quarter), jnp.float32),
            pltpu.VMEM((steps, 2, rows, quarter), jnp.float32),
            pltpu.VMEM((steps, 2, 2, rows, quarter), jnp.float32),
            pltpu.VMEM((steps, rows, quarter), dt),
            pltpu.VMEM((steps, rows, quarter), dt),
            pltpu.SemaphoreType.DMA((6,)),
            pltpu.SemaphoreType.DMA((2,)),
            pltpu.SemaphoreType.DMA((COPIES,)),
            pltpu.SemaphoreType.DMA((COPIES,)),
            pltpu.SemaphoreType.DMA((3 * PIECES,)),
            pltpu.SemaphoreType.DMA((3 * PIECES,)),
        ],
        compiler_params=pltpu.CompilerParams(
            collective_id=0, has_side_effects=True, vmem_limit_bytes=42 * 1024 * 1024
        ),
        name="layer",
    )(held, swapped, tokens, logits, routes, w_gate, w_up, w_down)[:4]


def per_device(tokens, logits, routes, held, swapped, w_gate, w_up, w_down):
    mixed, *tiles = layer(held, swapped, tokens, logits, routes, w_gate[0], w_up[0], w_down[0])
    return (mixed, *(tile[None] for tile in tiles))


def solution(mesh):
    in_specs = (
        P(None, "exp", "attn"),
        P(None, "exp", None),
        P(None, "exp", None),
        P(),
        P(),
        P("exp", None, "attn"),
        P("exp", None, "attn"),
        P("exp", None, "attn"),
    )
    out_specs = (
        P(None, "exp", "attn"),
        P("exp", None, "attn"),
        P("exp", None, "attn"),
        P("exp", None, "attn"),
    )
    return jax.shard_map(
        per_device, mesh=mesh, in_specs=in_specs, out_specs=out_specs, check_vma=False
    )
```

```python
import functools

import jax
import jax.numpy as jnp
from jax import lax
from jax.experimental import pallas as pl
from jax.experimental.pallas import tpu as pltpu
from jax.sharding import PartitionSpec as P

RING = 4


def wrap(value):
    return lax.rem(value + RING, RING)


def place():
    attn = lax.axis_index("attn")
    exp = lax.axis_index("exp")
    z_hi, core = attn // 2, lax.rem(attn, 2)
    z_lo, y, x = exp // 16, lax.rem(exp // 4, 4), lax.rem(exp, 4)
    return z_hi, core, z_lo, y, x


def device(z_hi, core, z_lo, y, x):
    return {"attn": z_hi * 2 + core, "exp": z_lo * 16 + y * 4 + x}


def neighbours(z_hi, core, z_lo, y, x):
    z = z_hi * 2 + z_lo
    right_z, left_z = wrap(z + 1), wrap(z - 1)
    along_z = [device(n // 2, core, lax.rem(n, 2), y, x) for n in (right_z, left_z)]
    along_x = [device(z_hi, core, z_lo, y, n) for n in (wrap(x + 1), wrap(x - 1))]
    along_y = [device(z_hi, core, z_lo, n, x) for n in (wrap(y + 1), wrap(y - 1))]
    return along_z, along_x, along_y, device(z_hi, 1 - core, z_lo, y, x)


def greet(devices):
    barrier = pltpu.get_barrier_semaphore()
    for other in devices:
        pl.semaphore_signal(barrier, inc=1, device_id=other, device_id_type=pl.DeviceIdType.MESH)
    pl.semaphore_wait(barrier, len(devices))


class Sends:
    def __init__(self, send_sem, recv_sem):
        self.send_sem, self.recv_sem, self.copies = send_sem, recv_sem, []

    def __call__(self, src, dst, to):
        k = len(self.copies)
        copy = pltpu.make_async_remote_copy(
            src_ref=src,
            dst_ref=dst,
            send_sem=self.send_sem.at[k],
            recv_sem=self.recv_sem.at[k],
            device_id=to,
            device_id_type=pl.DeviceIdType.MESH,
        )
        copy.start()
        self.copies.append(copy)
        return copy


STEPS = 2
PIECES = 16
SLAB = 64
FIRST, EARLY, BETWEEN, LATE = 0, 30, 31, 46
COPIES = 6 + 12 + 12 + 16 + 8 + 2 * (2 + 4 + 2 + 2) + 2
TILES = 8
EXTRA = 128


def layer_kernel(
    held_ref, swapped_ref, tokens_ref, logits_ref, routes_ref, wg_ref, wu_ref, wd_ref,
    mixed_ref, og_ref, ou_ref, od_ref, all_ref,
    wg_v, wu_v, wd_v, tok_ref, tile_v, hall, relay, sel_v, wcol_v,
    hop0, got0, sum0, hop1, got1, sum1, last,
    local_sem, tile_sem, send_sem, recv_sem, swap_send, swap_recv,
):
    z_hi, core, z_lo, y, x = place()
    along_z, along_x, along_y, sibling = neighbours(z_hi, core, z_lo, y, x)
    partner = device(z_hi, core, 1 - z_lo, y, x)
    z = z_hi * 2 + z_lo
    attn = z_hi * 2 + core
    wide = tok_ref.shape[2]
    quarter = wide - EXTRA
    part = wg_ref.shape[1]
    send = Sends(send_sem, recv_sem)

    loads = [
        pltpu.make_async_copy(src, dst, local_sem.at[2 + k])
        for k, (src, dst) in enumerate(((wg_ref, wg_v), (wu_ref, wu_v), (wd_ref, wd_v)))
    ]
    tok_load = pltpu.make_async_copy(tokens_ref, tok_ref.at[:, :, pl.ds(0, quarter)], local_sem.at[5])
    for copy in [tok_load, *loads]:
        copy.start()
    greet(along_z + along_x + along_y + [sibling])

    swaps = []
    for src, dst in ((wg_ref, og_ref), (wu_ref, ou_ref), (wd_ref, od_ref)):
        size = src.shape[0] // PIECES
        for k in range(PIECES):
            n = len(swaps)
            swaps.append(
                pltpu.make_async_remote_copy(
                    src_ref=src.at[pl.ds(k * size, size)],
                    dst_ref=dst.at[pl.ds(k * size, size)],
                    send_sem=swap_send.at[n],
                    recv_sem=swap_recv.at[n],
                    device_id=partner,
                    device_id_type=pl.DeviceIdType.MESH,
                )
            )
    begun = [0]

    def swap_until(count):
        for copy in swaps[begun[0] : count]:
            copy.start()
        begun[0] = max(begun[0], count)

    def cols(high):
        return pl.ds(pl.multiple_of((high * 2 + core) * wide, 128), wide)

    def spot(step, at):
        return all_ref.at[step, lax.rem(at, 2), y, x, :, cols(at // 2)]

    swap_until(FIRST)

    exp_count = held_ref.shape[0]
    top, here = logits_ref.shape[1:]
    lane_i = lax.broadcasted_iota(jnp.int32, (EXTRA, here), 0)
    expert_i = lax.rem(lane_i, exp_count)
    unit = lax.broadcasted_iota(jnp.int32, (here, here), 0) == lax.broadcasted_iota(jnp.int32, (here, here), 1)
    unit = jnp.where(unit, 1.0, 0.0).astype(jnp.bfloat16)
    for s in range(STEPS):
        score = 1.0 / (1.0 + jnp.exp(-logits_ref[s]))
        weight = score / jnp.sum(score, axis=0, keepdims=True)
        names = routes_ref[s]
        table = jnp.zeros(lane_i.shape, jnp.float32)
        for k in range(top):
            table = table + jnp.where(names[k : k + 1, :] == expert_i, weight[k : k + 1, :], 0.0)
        high = table.astype(jnp.bfloat16).astype(jnp.float32)
        middle = (table - high).astype(jnp.bfloat16).astype(jnp.float32)
        low = table - high - middle
        parts = jnp.where(lane_i < exp_count, high, jnp.where(lane_i < 2 * exp_count, middle, low))
        parts = jnp.where(lane_i < 3 * exp_count, parts, 0.0).astype(jnp.bfloat16)
        turned = lax.dot_general(unit, parts, (((1,), (1,)), ((), ())), preferred_element_type=jnp.float32)
        tok_ref[s, :, quarter:wide] = turned.astype(jnp.bfloat16)
    tok_load.wait()

    own = [pltpu.make_async_copy(tok_ref.at[s], spot(s, z), local_sem.at[s]) for s in range(STEPS)]
    for copy in own:
        copy.start()
    beyond = wrap(z + 2 * z_lo - 1)
    beyond_device = device(beyond // 2, core, lax.rem(beyond, 2), y, x)
    near = [send(tok_ref.at[s], spot(s, z), partner) for s in range(STEPS)]
    swap_until(EARLY)
    rest = {s: [send(tok_ref.at[s], spot(s, z), beyond_device)] for s in range(STEPS)}
    pair = z + 1 - 2 * z_lo
    for s in range(STEPS):
        near[s].wait_recv()
        rest[s].append(send(spot(s, pair), spot(s, pair), beyond_device))

    def line(step, axis, at, high):
        if axis == "x":
            return all_ref.at[step, :, y, at, :, cols(high)]
        return all_ref.at[step, :, at, x, :, cols(high)]

    def sheet(step, axis, at, high):
        if axis == "x":
            return all_ref.at[step, :, :, at, :, cols(high)]
        return all_ref.at[step, :, at, :, :, cols(high)]

    along = {"x": along_x, "y": along_y}
    spot_on = {"x": x, "y": y}
    order = (("x", "y"), ("y", "x"))

    def start_ring(unit, step, axis):
        at = spot_on[axis]
        return {
            (d, high): send(unit(step, axis, at, high), unit(step, axis, at, high), along[axis][d])
            for high in range(2)
            for d in range(2)
        }

    def forward_ring(copies, unit, step, axis):
        at = spot_on[axis]
        out = []
        for d in range(2):
            origin = wrap(at - 1) if d == 0 else wrap(at + 1)
            copies[d, d].wait_recv()
            out.append(send(unit(step, axis, origin, d), unit(step, axis, origin, d), along[axis][d]))
        return out

    lines, line_forwards = {}, {}
    for s in range(STEPS):
        for copy in rest[s]:
            copy.wait_recv()
        own[s].wait()
        lines[s] = start_ring(line, s, order[s][0])
    for s in range(STEPS):
        line_forwards[s] = forward_ring(lines[s], line, s, order[s][0])
    sheets, sheet_forwards, shared = {}, {}, []
    for s in range(STEPS):
        lines[s][0, 1].wait_recv()
        lines[s][1, 0].wait_recv()
        for copy in line_forwards[s]:
            copy.wait_recv()
        sheets[s] = start_ring(sheet, s, order[s][1])

    def share(step, offset, high):
        axis = order[step][1]
        unit = sheet(step, axis, wrap(spot_on[axis] + offset), high)
        shared.append(send(unit, unit, sibling))

    for s in range(STEPS):
        for high in range(2):
            share(s, 0, high)
    for s in range(STEPS):
        sheet_forwards[s] = forward_ring(sheets[s], sheet, s, order[s][1])
        share(s, -1, 0)
        share(s, 1, 1)
    for s in range(STEPS):
        sheets[s][0, 1].wait_recv()
        share(s, -1, 1)
        sheets[s][1, 0].wait_recv()
        share(s, 1, 0)
    for s in range(STEPS):
        for d in range(2):
            sheet_forwards[s][d].wait_recv()
            share(s, 2, d)
    for copy in shared:
        copy.wait_recv()
    for copy in loads:
        copy.wait()

    def tile_copy(t, slot):
        src = all_ref.at[t // 4, lax.rem(t // 2, 2), pl.ds(lax.rem(t, 2) * 2, 2)]
        return pltpu.make_async_copy(src, tile_v.at[slot], tile_sem.at[slot])

    span = tile_v.shape[1] * tile_v.shape[2] * tile_v.shape[3]
    slots = span // 2
    block = tile_v.shape[3]
    own_expert = held_ref[lax.axis_index("exp")]
    pick_i = lax.broadcasted_iota(jnp.int32, (16, EXTRA), 1)
    pick = jnp.where(
        (lax.rem(pick_i, exp_count) == own_expert) & (pick_i < 3 * exp_count), 1.0, 0.0
    ).astype(jnp.bfloat16)

    tile_copy(0, 0).start()

    def gate_up(t, carry):
        slot = lax.rem(t, 2)
        tile_copy(t, slot).wait()

        @pl.when(t + 1 < TILES)
        def _():
            tile_copy(t + 1, 1 - slot).start()

        extra = tile_v[slot, :, :, :, quarter:wide].reshape(span, EXTRA)
        along_lanes = lax.dot_general(pick, extra, (((1,), (1,)), ((), ())), preferred_element_type=jnp.float32)
        mask = along_lanes > 0.0
        row_i = lax.broadcasted_iota(jnp.int32, (span, span), 0)
        col_i = lax.broadcasted_iota(jnp.int32, (span, span), 1)
        upto = jnp.where((row_i // block == col_i // block) & (row_i <= col_i), 1.0, 0.0).astype(jnp.bfloat16)
        count = jnp.dot(
            jnp.where(mask, 1.0, 0.0).astype(jnp.bfloat16), upto, preferred_element_type=jnp.float32
        )
        base = lax.broadcasted_iota(jnp.int32, count.shape, 1) // block * (block // 2) - 1
        where_to = jnp.where(mask, count + base.astype(jnp.float32), -1.0)[0:1, :]
        slot_i = lax.broadcasted_iota(jnp.int32, (slots, span), 0).astype(jnp.float32)
        sel = jnp.where(slot_i == where_to, 1.0, 0.0).astype(jnp.bfloat16)
        sel_v[t] = sel
        wcol = jnp.sum(extra.astype(jnp.float32) * pick[0:1].astype(jnp.float32), axis=1, keepdims=True)
        wcol_v[t] = jnp.broadcast_to(2.5 * wcol, (span, 128))
        gate = jnp.zeros((slots, part), jnp.float32)
        upper = jnp.zeros((slots, part), jnp.float32)
        for q in range(4):
            rows = tile_v[slot, :, :, :, q * wide : q * wide + quarter].reshape(span, quarter)
            served = jnp.dot(sel, rows, preferred_element_type=jnp.float32).astype(jnp.bfloat16)
            w = pl.ds(q * quarter, quarter)
            gate = gate + jnp.dot(served, wg_v[w, :], preferred_element_type=jnp.float32)
            upper = upper + jnp.dot(served, wu_v[w, :], preferred_element_type=jnp.float32)
        act = gate / (1.0 + jnp.exp(-gate)) * upper
        hall[attn, t] = act.astype(jnp.bfloat16)
        return carry

    lax.fori_loop(0, TILES, gate_up, 0)

    half = [pl.ds(0, TILES // 2), pl.ds(TILES // 2, TILES // 2)]
    hops = [send(hall.at[attn, half[d]], relay.at[d], along_z[d]) for d in range(2)]
    to_core = [send(hall.at[attn], hall.at[attn], sibling)]
    swap_until(BETWEEN)
    far = []
    for d in range(2):
        hops[d].wait_recv()
        origin = (wrap(z - 1) if d == 0 else wrap(z + 1)) // 2 * 2 + core
        far.append(send(relay.at[d], hall.at[origin, half[d]], along_z[d]))
    swap_until(LATE)
    opposite = (1 - z_hi) * 2 + core
    for d in range(2):
        far[d].wait_recv()
        to_core.append(send(hall.at[opposite, half[d]], hall.at[opposite, half[d]], sibling))
    for copy in to_core:
        copy.wait_recv()

    def down(step, t, carry):
        total = jnp.zeros((slots, quarter), jnp.float32)
        for a in range(4):
            total = total + jnp.dot(
                hall[a, t], wd_v[pl.ds(a * part, part), :], preferred_element_type=jnp.float32
            )
        produced = total.astype(jnp.bfloat16)
        spread = lax.dot_general(
            sel_v[t], produced, (((0,), (0,)), ((), ())), preferred_element_type=jnp.float32
        )
        scaled = (wcol_v[t][:, 0:1] * spread).astype(jnp.bfloat16)
        scaled = scaled.reshape(2, RING, block, quarter)
        low = lax.rem(t // 2, 2)
        for k in range(2):
            row = lax.rem(t, 2) * 2 + k
            if step == 0:
                tile_v[0, low, :, :, pl.ds(pl.multiple_of(row * quarter, 128), quarter)] = scaled[k]
            else:
                for i in range(RING):
                    tile_v[1, low, row, :, i * quarter : (i + 1) * quarter] = scaled[k, i]
        return carry

    for step in range(STEPS):
        lax.fori_loop(step * TILES // 2, (step + 1) * TILES // 2, functools.partial(down, step), 0)

    flow = (("y", "x"), ("x", "y"))

    def lane(step, at):
        return tile_v.at[step, :, :, :, pl.ds(pl.multiple_of(at * quarter, 128), quarter)]

    hops, fulls = {}, {}
    for s in range(STEPS):
        axis = flow[s][0]
        at = spot_on[axis]
        hops[s] = [send(lane(s, wrap(at + 2)).at[d], hop0.at[s, d], along[axis][d]) for d in range(2)]
    for s in range(STEPS):
        axis = flow[s][0]
        at = spot_on[axis]
        for d in range(2):
            target = wrap(at + 1) if d == 0 else wrap(at - 1)
            fulls[s, d] = [send(lane(s, target).at[1 - d], got0.at[s, d, 1 - d], along[axis][d])]
    for s in range(STEPS):
        axis = flow[s][0]
        at = spot_on[axis]
        for d in range(2):
            target = wrap(at + 1) if d == 0 else wrap(at - 1)
            hops[s][d].wait_recv()
            mine = lane(s, target)

            @pl.loop(0, RING)
            def _(i, mine=mine, s=s, d=d):
                total = mine[d, i].astype(jnp.float32) + hop0[s, d, i].astype(jnp.float32)
                hop0[s, d, i] = total.astype(jnp.bfloat16)

            fulls[s, d].append(send(hop0.at[s, d], got0.at[s, d, d], along[axis][d]))
    hops1, fulls1 = {}, {}
    for s in range(STEPS):
        at = spot_on[flow[s][0]]
        mine = lane(s, at)
        for d in range(2):
            for copy in fulls[s, d]:
                copy.wait_recv()

        @pl.loop(0, RING)
        def _(i, mine=mine, s=s):
            for h in range(2):
                total = mine[h, i].astype(jnp.float32)
                total = total + got0[s, 0, h, i].astype(jnp.float32)
                total = total + got0[s, 1, h, i].astype(jnp.float32)
                sum0[s, h, i] = total

        axis = flow[s][1]
        at = spot_on[axis]
        hops1[s] = [send(sum0.at[s, d, wrap(at + 2)], hop1.at[s, d], along[axis][d]) for d in range(2)]
    for s in range(STEPS):
        axis = flow[s][1]
        at = spot_on[axis]
        for d in range(2):
            target = wrap(at + 1) if d == 0 else wrap(at - 1)
            hops1[s][d].wait_recv()
            sum0[s, d, target] = sum0[s, d, target] + hop1[s, d]
            fulls1[s, d] = send(sum0.at[s, :, target], got1.at[s, d], along[axis][d])
    finals = []
    for s in range(STEPS):
        at = spot_on[flow[s][1]]
        for d in range(2):
            fulls1[s, d].wait_recv()
        away = 1 - z_lo
        sum1[s] = (sum0[s, away, at] + got1[s, 0, away] + got1[s, 1, away]).astype(jnp.bfloat16)
        finals.append(send(sum1.at[s], last.at[s], partner))
    swap_until(3 * PIECES)
    for s in range(STEPS):
        at = spot_on[flow[s][1]]
        finals[s].wait_recv()
        total = sum0[s, z_lo, at] + got1[s, 0, z_lo] + got1[s, 1, z_lo] + last[s].astype(jnp.float32)
        mixed_ref[s] = total.astype(jnp.bfloat16)
    flag = swapped_ref[lax.rem(lax.axis_index("exp"), swapped_ref.shape[0])]
    n = 0
    for dst, src in ((og_ref, wg_v), (ou_ref, wu_v), (od_ref, wd_v)):
        size = src.shape[0] // PIECES
        for k in range(PIECES):
            swaps[n].wait_recv()

            @pl.loop(0, size // SLAB)
            def _(i, dst=dst, src=src, k=k, size=size):
                at = pl.ds(pl.multiple_of(k * size + i * SLAB, SLAB), SLAB)
                trade = jnp.full((SLAB, src.shape[1]), flag, jnp.int32) == 1
                dst[at, :] = jnp.where(trade, dst[at, :], src[at, :])

            n += 1
    for copy in send.copies + swaps:
        copy.wait_send()


def layer(held, swapped, tokens, logits, routes, w_gate, w_up, w_down):
    steps, rows, quarter = tokens.shape
    wide = quarter + EXTRA
    dt = tokens.dtype
    part = w_gate.shape[1]
    plane = (2, RING, RING, rows)
    hbm = pl.BlockSpec(memory_space=pl.ANY)
    vmem = pl.BlockSpec(memory_space=pltpu.VMEM)
    smem = pl.BlockSpec(memory_space=pltpu.SMEM)
    like = lambda a: jax.ShapeDtypeStruct(a.shape, a.dtype)
    return pl.pallas_call(
        layer_kernel,
        out_shape=(
            jax.ShapeDtypeStruct((steps, rows, quarter), dt),
            like(w_gate),
            like(w_up),
            like(w_down),
            jax.ShapeDtypeStruct((steps, *plane, 4 * wide), dt),
        ),
        in_specs=[smem, smem, pl.BlockSpec(memory_space=pltpu.HBM), vmem, vmem, hbm, hbm, hbm],
        out_specs=(vmem, vmem, vmem, vmem, hbm),
        scratch_shapes=[
            pltpu.VMEM(w_gate.shape, dt),
            pltpu.VMEM(w_up.shape, dt),
            pltpu.VMEM(w_down.shape, dt),
            pltpu.VMEM((steps, rows, wide), dt),
            pltpu.VMEM((2, 2, RING, rows, 4 * wide), dt),
            pltpu.VMEM((4, TILES, 4 * rows, part), dt),
            pltpu.VMEM((2, TILES // 2, 4 * rows, part), dt),
            pltpu.VMEM((TILES, 4 * rows, 8 * rows), dt),
            pltpu.VMEM((TILES, 8 * rows, 128), jnp.float32),
            pltpu.VMEM((steps, 2, RING, rows, quarter), dt),
            pltpu.VMEM((steps, 2, 2, RING, rows, quarter), dt),
            pltpu.VMEM((steps, 2, RING, rows, quarter), jnp.float32),
            pltpu.VMEM((steps, 2, rows, quarter), jnp.float32),
            pltpu.VMEM((steps, 2, 2, rows, quarter), jnp.float32),
            pltpu.VMEM((steps, rows, quarter), dt),
            pltpu.VMEM((steps, rows, quarter), dt),
            pltpu.SemaphoreType.DMA((6,)),
            pltpu.SemaphoreType.DMA((2,)),
            pltpu.SemaphoreType.DMA((COPIES,)),
            pltpu.SemaphoreType.DMA((COPIES,)),
            pltpu.SemaphoreType.DMA((3 * PIECES,)),
            pltpu.SemaphoreType.DMA((3 * PIECES,)),
        ],
        compiler_params=pltpu.CompilerParams(
            collective_id=0, has_side_effects=True, vmem_limit_bytes=42 * 1024 * 1024
        ),
        name="layer",
    )(held, swapped, tokens, logits, routes, w_gate, w_up, w_down)[:4]


STORES = 2


def store_kernel(*refs):
    count = (len(refs) - 1) // 2
    sems = refs[-1]
    copies = []
    for k in range(count):
        src, dst = refs[k], refs[count + k]
        size = src.shape[0] // STORES
        for i in range(STORES):
            rows = pl.ds(i * size, size)
            copies.append(pltpu.make_async_copy(src.at[rows], dst.at[rows], sems.at[len(copies)]))
    for copy in copies:
        copy.start()
    for copy in copies:
        copy.wait()


def store(*arrays):
    return pl.pallas_call(
        store_kernel,
        out_shape=tuple(jax.ShapeDtypeStruct(a.shape, a.dtype) for a in arrays),
        in_specs=[pl.BlockSpec(memory_space=pltpu.VMEM)] * len(arrays),
        out_specs=(pl.BlockSpec(memory_space=pl.ANY),) * len(arrays),
        scratch_shapes=[pltpu.SemaphoreType.DMA((STORES * len(arrays),))],
        compiler_params=pltpu.CompilerParams(vmem_limit_bytes=16 * 1024 * 1024),
        name="store",
    )(*arrays)


def per_device(tokens, logits, routes, held, swapped, w_gate, w_up, w_down):
    by_choice = (jnp.swapaxes(logits, 1, 2), jnp.swapaxes(routes, 1, 2))
    mixed, *tiles = layer(held, swapped, tokens, *by_choice, w_gate[0], w_up[0], w_down[0])
    mixed, *tiles = store(mixed, *tiles)
    return (mixed, *(tile[None] for tile in tiles))


def solution(mesh):
    in_specs = (
        P(None, "exp", "attn"),
        P(None, "exp", None),
        P(None, "exp", None),
        P(),
        P(),
        P("exp", None, "attn"),
        P("exp", None, "attn"),
        P("exp", None, "attn"),
    )
    out_specs = (
        P(None, "exp", "attn"),
        P("exp", None, "attn"),
        P("exp", None, "attn"),
        P("exp", None, "attn"),
    )
    return jax.shard_map(
        per_device, mesh=mesh, in_specs=in_specs, out_specs=out_specs, check_vma=False
    )
```

```python
import functools

import jax
import jax.numpy as jnp
from jax import lax
from jax.experimental import pallas as pl
from jax.experimental.pallas import tpu as pltpu
from jax.sharding import PartitionSpec as P

RING = 4


def wrap(value):
    return lax.rem(value + RING, RING)


def place():
    attn = lax.axis_index("attn")
    exp = lax.axis_index("exp")
    z_hi, core = attn // 2, lax.rem(attn, 2)
    z_lo, y, x = exp // 16, lax.rem(exp // 4, 4), lax.rem(exp, 4)
    return z_hi, core, z_lo, y, x


def device(z_hi, core, z_lo, y, x):
    return {"attn": z_hi * 2 + core, "exp": z_lo * 16 + y * 4 + x}


def neighbours(z_hi, core, z_lo, y, x):
    z = z_hi * 2 + z_lo
    right_z, left_z = wrap(z + 1), wrap(z - 1)
    along_z = [device(n // 2, core, lax.rem(n, 2), y, x) for n in (right_z, left_z)]
    along_x = [device(z_hi, core, z_lo, y, n) for n in (wrap(x + 1), wrap(x - 1))]
    along_y = [device(z_hi, core, z_lo, n, x) for n in (wrap(y + 1), wrap(y - 1))]
    return along_z, along_x, along_y, device(z_hi, 1 - core, z_lo, y, x)


def greet(devices):
    barrier = pltpu.get_barrier_semaphore()
    for other in devices:
        pl.semaphore_signal(barrier, inc=1, device_id=other, device_id_type=pl.DeviceIdType.MESH)
    pl.semaphore_wait(barrier, len(devices))


class Sends:
    def __init__(self, send_sem, recv_sem):
        self.send_sem, self.recv_sem, self.copies = send_sem, recv_sem, []

    def __call__(self, src, dst, to):
        k = len(self.copies)
        copy = pltpu.make_async_remote_copy(
            src_ref=src,
            dst_ref=dst,
            send_sem=self.send_sem.at[k],
            recv_sem=self.recv_sem.at[k],
            device_id=to,
            device_id_type=pl.DeviceIdType.MESH,
        )
        copy.start()
        self.copies.append(copy)
        return copy


STEPS = 2
PIECES = 16
SLAB = 64
FIRST, EARLY, BETWEEN, LATE = 2, 28, 29, 48
COPIES = 6 + 12 + 12 + 16 + 8 + 2 * (2 + 4 + 2 + 2) + 2
TILES = 8
EXTRA = 128


def layer_kernel(
    held_ref, swapped_ref, tokens_ref, logits_hbm, routes_hbm, wg_ref, wu_ref, wd_ref,
    mixed_ref, og_ref, ou_ref, od_ref, all_ref,
    wg_v, wu_v, wd_v, logits_ref, routes_ref, tok_ref, tile_v, hall, relay, sel_v, wcol_v,
    hop0, got0, sum0, hop1, got1, sum1, last,
    local_sem, tile_sem, send_sem, recv_sem, swap_send, swap_recv,
):
    z_hi, core, z_lo, y, x = place()
    along_z, along_x, along_y, sibling = neighbours(z_hi, core, z_lo, y, x)
    partner = device(z_hi, core, 1 - z_lo, y, x)
    z = z_hi * 2 + z_lo
    attn = z_hi * 2 + core
    wide = tok_ref.shape[2]
    quarter = wide - EXTRA
    part = wg_ref.shape[1]
    send = Sends(send_sem, recv_sem)

    loads = [
        pltpu.make_async_copy(src, dst, local_sem.at[2 + k])
        for k, (src, dst) in enumerate(((wg_ref, wg_v), (wu_ref, wu_v), (wd_ref, wd_v)))
    ]
    tok_load = pltpu.make_async_copy(tokens_ref, tok_ref.at[:, :, pl.ds(0, quarter)], local_sem.at[5])
    route_loads = [
        pltpu.make_async_copy(logits_hbm, logits_ref, local_sem.at[6]),
        pltpu.make_async_copy(routes_hbm, routes_ref, local_sem.at[7]),
    ]
    for copy in [*route_loads, tok_load, *loads]:
        copy.start()
    greet(along_z + along_x + along_y + [sibling])

    swaps = []
    for src, dst in ((wg_ref, og_ref), (wu_ref, ou_ref), (wd_ref, od_ref)):
        size = src.shape[0] // PIECES
        for k in range(PIECES):
            n = len(swaps)
            swaps.append(
                pltpu.make_async_remote_copy(
                    src_ref=src.at[pl.ds(k * size, size)],
                    dst_ref=dst.at[pl.ds(k * size, size)],
                    send_sem=swap_send.at[n],
                    recv_sem=swap_recv.at[n],
                    device_id=partner,
                    device_id_type=pl.DeviceIdType.MESH,
                )
            )
    begun = [0]

    def swap_until(count):
        for copy in swaps[begun[0] : count]:
            copy.start()
        begun[0] = max(begun[0], count)

    def cols(high):
        return pl.ds(pl.multiple_of((high * 2 + core) * wide, 128), wide)

    def spot(step, at):
        return all_ref.at[step, lax.rem(at, 2), y, x, :, cols(at // 2)]

    swap_until(FIRST)

    for copy in route_loads:
        copy.wait()
    exp_count = held_ref.shape[0]
    top, here = logits_ref.shape[1:]
    lane_i = lax.broadcasted_iota(jnp.int32, (EXTRA, here), 0)
    expert_i = lax.rem(lane_i, exp_count)
    unit = lax.broadcasted_iota(jnp.int32, (here, here), 0) == lax.broadcasted_iota(jnp.int32, (here, here), 1)
    unit = jnp.where(unit, 1.0, 0.0).astype(jnp.bfloat16)
    for s in range(STEPS):
        score = 1.0 / (1.0 + jnp.exp(-logits_ref[s]))
        weight = score / jnp.sum(score, axis=0, keepdims=True)
        names = routes_ref[s]
        table = jnp.zeros(lane_i.shape, jnp.float32)
        for k in range(top):
            table = table + jnp.where(names[k : k + 1, :] == expert_i, weight[k : k + 1, :], 0.0)
        high = table.astype(jnp.bfloat16).astype(jnp.float32)
        middle = (table - high).astype(jnp.bfloat16).astype(jnp.float32)
        low = table - high - middle
        parts = jnp.where(lane_i < exp_count, high, jnp.where(lane_i < 2 * exp_count, middle, low))
        parts = jnp.where(lane_i < 3 * exp_count, parts, 0.0).astype(jnp.bfloat16)
        turned = lax.dot_general(unit, parts, (((1,), (1,)), ((), ())), preferred_element_type=jnp.float32)
        tok_ref[s, :, quarter:wide] = turned.astype(jnp.bfloat16)
    tok_load.wait()

    own = [pltpu.make_async_copy(tok_ref.at[s], spot(s, z), local_sem.at[s]) for s in range(STEPS)]
    for copy in own:
        copy.start()
    beyond = wrap(z + 2 * z_lo - 1)
    beyond_device = device(beyond // 2, core, lax.rem(beyond, 2), y, x)
    near = [send(tok_ref.at[s], spot(s, z), partner) for s in range(STEPS)]
    swap_until(EARLY)
    rest = {s: [send(tok_ref.at[s], spot(s, z), beyond_device)] for s in range(STEPS)}
    pair = z + 1 - 2 * z_lo
    for s in range(STEPS):
        near[s].wait_recv()
        rest[s].append(send(spot(s, pair), spot(s, pair), beyond_device))

    def line(step, axis, at, high):
        if axis == "x":
            return all_ref.at[step, :, y, at, :, cols(high)]
        return all_ref.at[step, :, at, x, :, cols(high)]

    def sheet(step, axis, at, high):
        if axis == "x":
            return all_ref.at[step, :, :, at, :, cols(high)]
        return all_ref.at[step, :, at, :, :, cols(high)]

    along = {"x": along_x, "y": along_y}
    spot_on = {"x": x, "y": y}
    order = (("x", "y"), ("y", "x"))

    def start_ring(unit, step, axis):
        at = spot_on[axis]
        return {
            (d, high): send(unit(step, axis, at, high), unit(step, axis, at, high), along[axis][d])
            for high in range(2)
            for d in range(2)
        }

    def forward_ring(copies, unit, step, axis):
        at = spot_on[axis]
        out = []
        for d in range(2):
            origin = wrap(at - 1) if d == 0 else wrap(at + 1)
            copies[d, d].wait_recv()
            out.append(send(unit(step, axis, origin, d), unit(step, axis, origin, d), along[axis][d]))
        return out

    lines, line_forwards = {}, {}
    for s in range(STEPS):
        for copy in rest[s]:
            copy.wait_recv()
        own[s].wait()
        lines[s] = start_ring(line, s, order[s][0])
    for s in range(STEPS):
        line_forwards[s] = forward_ring(lines[s], line, s, order[s][0])
    sheets, sheet_forwards, shared = {}, {}, []
    for s in range(STEPS):
        lines[s][0, 1].wait_recv()
        lines[s][1, 0].wait_recv()
        for copy in line_forwards[s]:
            copy.wait_recv()
        sheets[s] = start_ring(sheet, s, order[s][1])

    def share(step, offset, high):
        axis = order[step][1]
        unit = sheet(step, axis, wrap(spot_on[axis] + offset), high)
        shared.append(send(unit, unit, sibling))

    for s in range(STEPS):
        for high in range(2):
            share(s, 0, high)
    for s in range(STEPS):
        sheet_forwards[s] = forward_ring(sheets[s], sheet, s, order[s][1])
        share(s, -1, 0)
        share(s, 1, 1)
    for s in range(STEPS):
        sheets[s][0, 1].wait_recv()
        share(s, -1, 1)
        sheets[s][1, 0].wait_recv()
        share(s, 1, 0)
    for s in range(STEPS):
        for d in range(2):
            sheet_forwards[s][d].wait_recv()
            share(s, 2, d)
    for copy in shared:
        copy.wait_recv()
    for copy in loads:
        copy.wait()

    def tile_copy(t, slot):
        src = all_ref.at[t // 4, lax.rem(t // 2, 2), pl.ds(lax.rem(t, 2) * 2, 2)]
        return pltpu.make_async_copy(src, tile_v.at[slot], tile_sem.at[slot])

    span = tile_v.shape[1] * tile_v.shape[2] * tile_v.shape[3]
    slots = span // 2
    block = tile_v.shape[3]
    own_expert = held_ref[lax.axis_index("exp")]
    pick_i = lax.broadcasted_iota(jnp.int32, (16, EXTRA), 1)
    pick = jnp.where(
        (lax.rem(pick_i, exp_count) == own_expert) & (pick_i < 3 * exp_count), 1.0, 0.0
    ).astype(jnp.bfloat16)

    tile_copy(0, 0).start()

    def gate_up(t, carry):
        slot = lax.rem(t, 2)
        tile_copy(t, slot).wait()

        @pl.when(t + 1 < TILES)
        def _():
            tile_copy(t + 1, 1 - slot).start()

        extra = tile_v[slot, :, :, :, quarter:wide].reshape(span, EXTRA)
        along_lanes = lax.dot_general(pick, extra, (((1,), (1,)), ((), ())), preferred_element_type=jnp.float32)
        mask = along_lanes > 0.0
        row_i = lax.broadcasted_iota(jnp.int32, (span, span), 0)
        col_i = lax.broadcasted_iota(jnp.int32, (span, span), 1)
        upto = jnp.where((row_i // block == col_i // block) & (row_i <= col_i), 1.0, 0.0).astype(jnp.bfloat16)
        count = jnp.dot(
            jnp.where(mask, 1.0, 0.0).astype(jnp.bfloat16), upto, preferred_element_type=jnp.float32
        )
        base = lax.broadcasted_iota(jnp.int32, count.shape, 1) // block * (block // 2) - 1
        where_to = jnp.where(mask, count + base.astype(jnp.float32), -1.0)[0:1, :]
        slot_i = lax.broadcasted_iota(jnp.int32, (slots, span), 0).astype(jnp.float32)
        sel = jnp.where(slot_i == where_to, 1.0, 0.0).astype(jnp.bfloat16)
        sel_v[t] = sel
        wcol = jnp.sum(extra.astype(jnp.float32) * pick[0:1].astype(jnp.float32), axis=1, keepdims=True)
        wcol_v[t] = jnp.broadcast_to(2.5 * wcol, (span, 128))
        gate = jnp.zeros((slots, part), jnp.float32)
        upper = jnp.zeros((slots, part), jnp.float32)
        for q in range(4):
            rows = tile_v[slot, :, :, :, q * wide : q * wide + quarter].reshape(span, quarter)
            served = jnp.dot(sel, rows, preferred_element_type=jnp.float32).astype(jnp.bfloat16)
            w = pl.ds(q * quarter, quarter)
            gate = gate + jnp.dot(served, wg_v[w, :], preferred_element_type=jnp.float32)
            upper = upper + jnp.dot(served, wu_v[w, :], preferred_element_type=jnp.float32)
        act = gate / (1.0 + jnp.exp(-gate)) * upper
        hall[attn, t] = act.astype(jnp.bfloat16)
        return carry

    lax.fori_loop(0, TILES, gate_up, 0)

    half = [pl.ds(0, TILES // 2), pl.ds(TILES // 2, TILES // 2)]
    hops = [send(hall.at[attn, half[d]], relay.at[d], along_z[d]) for d in range(2)]
    to_core = [send(hall.at[attn], hall.at[attn], sibling)]
    swap_until(BETWEEN)
    far = []
    for d in range(2):
        hops[d].wait_recv()
        origin = (wrap(z - 1) if d == 0 else wrap(z + 1)) // 2 * 2 + core
        far.append(send(relay.at[d], hall.at[origin, half[d]], along_z[d]))
    swap_until(LATE)
    opposite = (1 - z_hi) * 2 + core
    for d in range(2):
        far[d].wait_recv()
        to_core.append(send(hall.at[opposite, half[d]], hall.at[opposite, half[d]], sibling))
    for copy in to_core:
        copy.wait_recv()

    def down(step, t, carry):
        total = jnp.zeros((slots, quarter), jnp.float32)
        for a in range(4):
            total = total + jnp.dot(
                hall[a, t], wd_v[pl.ds(a * part, part), :], preferred_element_type=jnp.float32
            )
        produced = total.astype(jnp.bfloat16)
        spread = lax.dot_general(
            sel_v[t], produced, (((0,), (0,)), ((), ())), preferred_element_type=jnp.float32
        )
        scaled = (wcol_v[t][:, 0:1] * spread).astype(jnp.bfloat16)
        scaled = scaled.reshape(2, RING, block, quarter)
        low = lax.rem(t // 2, 2)
        for k in range(2):
            row = lax.rem(t, 2) * 2 + k
            if step == 0:
                tile_v[0, low, :, :, pl.ds(pl.multiple_of(row * quarter, 128), quarter)] = scaled[k]
            else:
                for i in range(RING):
                    tile_v[1, low, row, :, i * quarter : (i + 1) * quarter] = scaled[k, i]
        return carry

    for step in range(STEPS):
        lax.fori_loop(step * TILES // 2, (step + 1) * TILES // 2, functools.partial(down, step), 0)

    flow = (("y", "x"), ("x", "y"))

    def lane(step, at):
        return tile_v.at[step, :, :, :, pl.ds(pl.multiple_of(at * quarter, 128), quarter)]

    hops, fulls = {}, {}
    for s in range(STEPS):
        axis = flow[s][0]
        at = spot_on[axis]
        hops[s] = [send(lane(s, wrap(at + 2)).at[d], hop0.at[s, d], along[axis][d]) for d in range(2)]
    for s in range(STEPS):
        axis = flow[s][0]
        at = spot_on[axis]
        for d in range(2):
            target = wrap(at + 1) if d == 0 else wrap(at - 1)
            fulls[s, d] = [send(lane(s, target).at[1 - d], got0.at[s, d, 1 - d], along[axis][d])]
    for s in range(STEPS):
        axis = flow[s][0]
        at = spot_on[axis]
        for d in range(2):
            target = wrap(at + 1) if d == 0 else wrap(at - 1)
            hops[s][d].wait_recv()
            mine = lane(s, target)

            @pl.loop(0, RING)
            def _(i, mine=mine, s=s, d=d):
                total = mine[d, i].astype(jnp.float32) + hop0[s, d, i].astype(jnp.float32)
                hop0[s, d, i] = total.astype(jnp.bfloat16)

            fulls[s, d].append(send(hop0.at[s, d], got0.at[s, d, d], along[axis][d]))
    hops1, fulls1 = {}, {}
    for s in range(STEPS):
        at = spot_on[flow[s][0]]
        mine = lane(s, at)
        for d in range(2):
            for copy in fulls[s, d]:
                copy.wait_recv()

        @pl.loop(0, RING)
        def _(i, mine=mine, s=s):
            for h in range(2):
                total = mine[h, i].astype(jnp.float32)
                total = total + got0[s, 0, h, i].astype(jnp.float32)
                total = total + got0[s, 1, h, i].astype(jnp.float32)
                sum0[s, h, i] = total

        axis = flow[s][1]
        at = spot_on[axis]
        hops1[s] = [send(sum0.at[s, d, wrap(at + 2)], hop1.at[s, d], along[axis][d]) for d in range(2)]
    for s in range(STEPS):
        axis = flow[s][1]
        at = spot_on[axis]
        for d in range(2):
            target = wrap(at + 1) if d == 0 else wrap(at - 1)
            hops1[s][d].wait_recv()
            sum0[s, d, target] = sum0[s, d, target] + hop1[s, d]
            fulls1[s, d] = send(sum0.at[s, :, target], got1.at[s, d], along[axis][d])
    finals = []
    for s in range(STEPS):
        at = spot_on[flow[s][1]]
        for d in range(2):
            fulls1[s, d].wait_recv()
        away = 1 - z_lo
        sum1[s] = (sum0[s, away, at] + got1[s, 0, away] + got1[s, 1, away]).astype(jnp.bfloat16)
        finals.append(send(sum1.at[s], last.at[s], partner))
    swap_until(3 * PIECES)

    flag = swapped_ref[lax.rem(lax.axis_index("exp"), swapped_ref.shape[0])]
    settled = [0]

    def settle(count):
        while settled[0] < count:
            n = settled[0]
            dst, src = ((og_ref, wg_v), (ou_ref, wu_v), (od_ref, wd_v))[n // PIECES]
            size = src.shape[0] // PIECES
            start = n % PIECES * size
            swaps[n].wait_recv()

            @pl.loop(0, size // SLAB)
            def _(i, dst=dst, src=src, start=start):
                at = pl.ds(pl.multiple_of(start + i * SLAB, SLAB), SLAB)
                trade = jnp.full((SLAB, src.shape[1]), flag, jnp.int32) == 1
                dst[at, :] = jnp.where(trade, dst[at, :], src[at, :])

            settled[0] += 1

    settle(LATE - 2)
    for s in range(STEPS):
        at = spot_on[flow[s][1]]
        finals[s].wait_recv()
        total = sum0[s, z_lo, at] + got1[s, 0, z_lo] + got1[s, 1, z_lo] + last[s].astype(jnp.float32)
        mixed_ref[s] = total.astype(jnp.bfloat16)
    settle(3 * PIECES)
    for copy in send.copies + swaps:
        copy.wait_send()


def layer(held, swapped, tokens, logits, routes, w_gate, w_up, w_down):
    steps, rows, quarter = tokens.shape
    wide = quarter + EXTRA
    dt = tokens.dtype
    part = w_gate.shape[1]
    plane = (2, RING, RING, rows)
    hbm = pl.BlockSpec(memory_space=pl.ANY)
    vmem = pl.BlockSpec(memory_space=pltpu.VMEM)
    smem = pl.BlockSpec(memory_space=pltpu.SMEM)
    like = lambda a: jax.ShapeDtypeStruct(a.shape, a.dtype)
    return pl.pallas_call(
        layer_kernel,
        out_shape=(
            jax.ShapeDtypeStruct((steps, rows, quarter), dt),
            like(w_gate),
            like(w_up),
            like(w_down),
            jax.ShapeDtypeStruct((steps, *plane, 4 * wide), dt),
        ),
        in_specs=[smem, smem, *[pl.BlockSpec(memory_space=pltpu.HBM)] * 3, hbm, hbm, hbm],
        out_specs=(vmem, vmem, vmem, vmem, hbm),
        scratch_shapes=[
            pltpu.VMEM(w_gate.shape, dt),
            pltpu.VMEM(w_up.shape, dt),
            pltpu.VMEM(w_down.shape, dt),
            pltpu.VMEM(logits.shape, logits.dtype),
            pltpu.VMEM(routes.shape, routes.dtype),
            pltpu.VMEM((steps, rows, wide), dt),
            pltpu.VMEM((2, 2, RING, rows, 4 * wide), dt),
            pltpu.VMEM((4, TILES, 4 * rows, part), dt),
            pltpu.VMEM((2, TILES // 2, 4 * rows, part), dt),
            pltpu.VMEM((TILES, 4 * rows, 8 * rows), dt),
            pltpu.VMEM((TILES, 8 * rows, 128), jnp.float32),
            pltpu.VMEM((steps, 2, RING, rows, quarter), dt),
            pltpu.VMEM((steps, 2, 2, RING, rows, quarter), dt),
            pltpu.VMEM((steps, 2, RING, rows, quarter), jnp.float32),
            pltpu.VMEM((steps, 2, rows, quarter), jnp.float32),
            pltpu.VMEM((steps, 2, 2, rows, quarter), jnp.float32),
            pltpu.VMEM((steps, rows, quarter), dt),
            pltpu.VMEM((steps, rows, quarter), dt),
            pltpu.SemaphoreType.DMA((8,)),
            pltpu.SemaphoreType.DMA((2,)),
            pltpu.SemaphoreType.DMA((COPIES,)),
            pltpu.SemaphoreType.DMA((COPIES,)),
            pltpu.SemaphoreType.DMA((3 * PIECES,)),
            pltpu.SemaphoreType.DMA((3 * PIECES,)),
        ],
        compiler_params=pltpu.CompilerParams(
            collective_id=0, has_side_effects=True, vmem_limit_bytes=42 * 1024 * 1024
        ),
        name="layer",
    )(held, swapped, tokens, logits, routes, w_gate, w_up, w_down)[:4]


STORES = 2


def store_kernel(*refs):
    count = (len(refs) - 1) // 2
    sems = refs[-1]
    copies = []
    for k in range(count):
        src, dst = refs[k], refs[count + k]
        size = src.shape[0] // STORES
        for i in range(STORES):
            rows = pl.ds(i * size, size)
            copies.append(pltpu.make_async_copy(src.at[rows], dst.at[rows], sems.at[len(copies)]))
    for copy in copies:
        copy.start()
    for copy in copies:
        copy.wait()


def store(*arrays):
    return pl.pallas_call(
        store_kernel,
        out_shape=tuple(jax.ShapeDtypeStruct(a.shape, a.dtype) for a in arrays),
        in_specs=[pl.BlockSpec(memory_space=pltpu.VMEM)] * len(arrays),
        out_specs=(pl.BlockSpec(memory_space=pl.ANY),) * len(arrays),
        scratch_shapes=[pltpu.SemaphoreType.DMA((STORES * len(arrays),))],
        compiler_params=pltpu.CompilerParams(vmem_limit_bytes=16 * 1024 * 1024),
        name="store",
    )(*arrays)


def per_device(tokens, logits, routes, held, swapped, w_gate, w_up, w_down):
    by_choice = (jnp.swapaxes(logits, 1, 2), jnp.swapaxes(routes, 1, 2))
    tokens, *by_choice = (pltpu.with_memory_space_constraint(a, pltpu.HBM) for a in (tokens, *by_choice))
    mixed, *tiles = layer(held, swapped, tokens, *by_choice, w_gate[0], w_up[0], w_down[0])
    mixed, *tiles = store(mixed, *tiles)
    return (mixed, *(tile[None] for tile in tiles))


def solution(mesh):
    in_specs = (
        P(None, "exp", "attn"),
        P(None, "exp", None),
        P(None, "exp", None),
        P(),
        P(),
        P("exp", None, "attn"),
        P("exp", None, "attn"),
        P("exp", None, "attn"),
    )
    out_specs = (
        P(None, "exp", "attn"),
        P("exp", None, "attn"),
        P("exp", None, "attn"),
        P("exp", None, "attn"),
    )
    return jax.shard_map(
        per_device, mesh=mesh, in_specs=in_specs, out_specs=out_specs, check_vma=False
    )
```

```python
import functools

import jax
import jax.numpy as jnp
from jax import lax
from jax.experimental import pallas as pl
from jax.experimental.pallas import tpu as pltpu
from jax.sharding import PartitionSpec as P

RING = 4


def wrap(value):
    return lax.rem(value + RING, RING)


def place():
    attn = lax.axis_index("attn")
    exp = lax.axis_index("exp")
    z_hi, core = attn // 2, lax.rem(attn, 2)
    z_lo, y, x = exp // 16, lax.rem(exp // 4, 4), lax.rem(exp, 4)
    return z_hi, core, z_lo, y, x


def device(z_hi, core, z_lo, y, x):
    return {"attn": z_hi * 2 + core, "exp": z_lo * 16 + y * 4 + x}


def neighbours(z_hi, core, z_lo, y, x):
    z = z_hi * 2 + z_lo
    right_z, left_z = wrap(z + 1), wrap(z - 1)
    along_z = [device(n // 2, core, lax.rem(n, 2), y, x) for n in (right_z, left_z)]
    along_x = [device(z_hi, core, z_lo, y, n) for n in (wrap(x + 1), wrap(x - 1))]
    along_y = [device(z_hi, core, z_lo, n, x) for n in (wrap(y + 1), wrap(y - 1))]
    return along_z, along_x, along_y, device(z_hi, 1 - core, z_lo, y, x)


def greet(devices):
    barrier = pltpu.get_barrier_semaphore()
    for other in devices:
        pl.semaphore_signal(barrier, inc=1, device_id=other, device_id_type=pl.DeviceIdType.MESH)
    pl.semaphore_wait(barrier, len(devices))


class Sends:
    def __init__(self, send_sem, recv_sem):
        self.send_sem, self.recv_sem, self.copies = send_sem, recv_sem, []

    def __call__(self, src, dst, to):
        k = len(self.copies)
        copy = pltpu.make_async_remote_copy(
            src_ref=src,
            dst_ref=dst,
            send_sem=self.send_sem.at[k],
            recv_sem=self.recv_sem.at[k],
            device_id=to,
            device_id_type=pl.DeviceIdType.MESH,
        )
        copy.start()
        self.copies.append(copy)
        return copy


STEPS = 2
PIECES = 16
SLAB = 64
FIRST, EARLY, BETWEEN, LATE = 2, 28, 29, 48
COPIES = 6 + 12 + 12 + 16 + 8 + 2 * (2 + 4 + 2 + 2) + 2
TILES = 8
EXTRA = 128


def layer_kernel(
    held_hbm, swapped_hbm, tokens_ref, logits_hbm, routes_hbm, wg_ref, wu_ref, wd_ref,
    mixed_ref, og_ref, ou_ref, od_ref, all_ref,
    wg_v, wu_v, wd_v, held_ref, swapped_ref, logits_ref, routes_ref, tok_ref, tile_v, hall, relay, sel_v, wcol_v,
    hop0, got0, sum0, hop1, got1, sum1, last,
    local_sem, tile_sem, send_sem, recv_sem, swap_send, swap_recv,
):
    z_hi, core, z_lo, y, x = place()
    along_z, along_x, along_y, sibling = neighbours(z_hi, core, z_lo, y, x)
    partner = device(z_hi, core, 1 - z_lo, y, x)
    z = z_hi * 2 + z_lo
    attn = z_hi * 2 + core
    wide = tok_ref.shape[2]
    quarter = wide - EXTRA
    part = wg_ref.shape[1]
    send = Sends(send_sem, recv_sem)

    loads = [
        pltpu.make_async_copy(src, dst, local_sem.at[2 + k])
        for k, (src, dst) in enumerate(((wg_ref, wg_v), (wu_ref, wu_v), (wd_ref, wd_v)))
    ]
    tok_load = pltpu.make_async_copy(tokens_ref, tok_ref.at[:, :, pl.ds(0, quarter)], local_sem.at[5])
    route_loads = [
        pltpu.make_async_copy(logits_hbm, logits_ref, local_sem.at[6]),
        pltpu.make_async_copy(routes_hbm, routes_ref, local_sem.at[7]),
        pltpu.make_async_copy(held_hbm, held_ref, local_sem.at[8]),
        pltpu.make_async_copy(swapped_hbm, swapped_ref, local_sem.at[9]),
    ]
    for copy in [*route_loads, tok_load, *loads]:
        copy.start()
    greet(along_z + along_x + along_y + [sibling])

    swaps = []
    for src, dst in ((wg_ref, og_ref), (wu_ref, ou_ref), (wd_ref, od_ref)):
        size = src.shape[0] // PIECES
        for k in range(PIECES):
            n = len(swaps)
            swaps.append(
                pltpu.make_async_remote_copy(
                    src_ref=src.at[pl.ds(k * size, size)],
                    dst_ref=dst.at[pl.ds(k * size, size)],
                    send_sem=swap_send.at[n],
                    recv_sem=swap_recv.at[n],
                    device_id=partner,
                    device_id_type=pl.DeviceIdType.MESH,
                )
            )
    begun = [0]

    def swap_until(count):
        for copy in swaps[begun[0] : count]:
            copy.start()
        begun[0] = max(begun[0], count)

    def cols(high):
        return pl.ds(pl.multiple_of((high * 2 + core) * wide, 128), wide)

    def spot(step, at):
        return all_ref.at[step, lax.rem(at, 2), y, x, :, cols(at // 2)]

    swap_until(FIRST)

    for copy in route_loads:
        copy.wait()
    exp_count = held_ref.shape[0]
    top, here = logits_ref.shape[1:]
    lane_i = lax.broadcasted_iota(jnp.int32, (EXTRA, here), 0)
    expert_i = lax.rem(lane_i, exp_count)
    unit = lax.broadcasted_iota(jnp.int32, (here, here), 0) == lax.broadcasted_iota(jnp.int32, (here, here), 1)
    unit = jnp.where(unit, 1.0, 0.0).astype(jnp.bfloat16)
    for s in range(STEPS):
        score = 1.0 / (1.0 + jnp.exp(-logits_ref[s]))
        weight = score / jnp.sum(score, axis=0, keepdims=True)
        names = routes_ref[s]
        table = jnp.zeros(lane_i.shape, jnp.float32)
        for k in range(top):
            table = table + jnp.where(names[k : k + 1, :] == expert_i, weight[k : k + 1, :], 0.0)
        high = table.astype(jnp.bfloat16).astype(jnp.float32)
        middle = (table - high).astype(jnp.bfloat16).astype(jnp.float32)
        low = table - high - middle
        parts = jnp.where(lane_i < exp_count, high, jnp.where(lane_i < 2 * exp_count, middle, low))
        parts = jnp.where(lane_i < 3 * exp_count, parts, 0.0).astype(jnp.bfloat16)
        turned = lax.dot_general(unit, parts, (((1,), (1,)), ((), ())), preferred_element_type=jnp.float32)
        tok_ref[s, :, quarter:wide] = turned.astype(jnp.bfloat16)
    tok_load.wait()

    own = [pltpu.make_async_copy(tok_ref.at[s], spot(s, z), local_sem.at[s]) for s in range(STEPS)]
    for copy in own:
        copy.start()
    beyond = wrap(z + 2 * z_lo - 1)
    beyond_device = device(beyond // 2, core, lax.rem(beyond, 2), y, x)
    near = [send(tok_ref.at[s], spot(s, z), partner) for s in range(STEPS)]
    swap_until(EARLY)
    rest = {s: [send(tok_ref.at[s], spot(s, z), beyond_device)] for s in range(STEPS)}
    pair = z + 1 - 2 * z_lo
    for s in range(STEPS):
        near[s].wait_recv()
        rest[s].append(send(spot(s, pair), spot(s, pair), beyond_device))

    def line(step, axis, at, high):
        if axis == "x":
            return all_ref.at[step, :, y, at, :, cols(high)]
        return all_ref.at[step, :, at, x, :, cols(high)]

    def sheet(step, axis, at, high):
        if axis == "x":
            return all_ref.at[step, :, :, at, :, cols(high)]
        return all_ref.at[step, :, at, :, :, cols(high)]

    along = {"x": along_x, "y": along_y}
    spot_on = {"x": x, "y": y}
    order = (("x", "y"), ("y", "x"))

    def start_ring(unit, step, axis):
        at = spot_on[axis]
        return {
            (d, high): send(unit(step, axis, at, high), unit(step, axis, at, high), along[axis][d])
            for high in range(2)
            for d in range(2)
        }

    def forward_ring(copies, unit, step, axis):
        at = spot_on[axis]
        out = []
        for d in range(2):
            origin = wrap(at - 1) if d == 0 else wrap(at + 1)
            copies[d, d].wait_recv()
            out.append(send(unit(step, axis, origin, d), unit(step, axis, origin, d), along[axis][d]))
        return out

    lines, line_forwards = {}, {}
    for s in range(STEPS):
        for copy in rest[s]:
            copy.wait_recv()
        own[s].wait()
        lines[s] = start_ring(line, s, order[s][0])
    for s in range(STEPS):
        line_forwards[s] = forward_ring(lines[s], line, s, order[s][0])
    sheets, sheet_forwards, shared = {}, {}, []
    for s in range(STEPS):
        lines[s][0, 1].wait_recv()
        lines[s][1, 0].wait_recv()
        for copy in line_forwards[s]:
            copy.wait_recv()
        sheets[s] = start_ring(sheet, s, order[s][1])

    def share(step, offset, high):
        axis = order[step][1]
        unit = sheet(step, axis, wrap(spot_on[axis] + offset), high)
        shared.append(send(unit, unit, sibling))

    for s in range(STEPS):
        for high in range(2):
            share(s, 0, high)
    for s in range(STEPS):
        sheet_forwards[s] = forward_ring(sheets[s], sheet, s, order[s][1])
        share(s, -1, 0)
        share(s, 1, 1)
    for s in range(STEPS):
        sheets[s][0, 1].wait_recv()
        share(s, -1, 1)
        sheets[s][1, 0].wait_recv()
        share(s, 1, 0)
    for s in range(STEPS):
        for d in range(2):
            sheet_forwards[s][d].wait_recv()
            share(s, 2, d)
    for copy in shared:
        copy.wait_recv()
    for copy in loads:
        copy.wait()

    def tile_copy(t, slot):
        src = all_ref.at[t // 4, lax.rem(t // 2, 2), pl.ds(lax.rem(t, 2) * 2, 2)]
        return pltpu.make_async_copy(src, tile_v.at[slot], tile_sem.at[slot])

    span = tile_v.shape[1] * tile_v.shape[2] * tile_v.shape[3]
    slots = span // 2
    block = tile_v.shape[3]
    own_expert = held_ref[lax.axis_index("exp")]
    pick_i = lax.broadcasted_iota(jnp.int32, (16, EXTRA), 1)
    pick = jnp.where(
        (lax.rem(pick_i, exp_count) == own_expert) & (pick_i < 3 * exp_count), 1.0, 0.0
    ).astype(jnp.bfloat16)

    tile_copy(0, 0).start()

    def gate_up(t, carry):
        slot = lax.rem(t, 2)
        tile_copy(t, slot).wait()

        @pl.when(t + 1 < TILES)
        def _():
            tile_copy(t + 1, 1 - slot).start()

        extra = tile_v[slot, :, :, :, quarter:wide].reshape(span, EXTRA)
        along_lanes = lax.dot_general(pick, extra, (((1,), (1,)), ((), ())), preferred_element_type=jnp.float32)
        mask = along_lanes > 0.0
        row_i = lax.broadcasted_iota(jnp.int32, (span, span), 0)
        col_i = lax.broadcasted_iota(jnp.int32, (span, span), 1)
        upto = jnp.where((row_i // block == col_i // block) & (row_i <= col_i), 1.0, 0.0).astype(jnp.bfloat16)
        count = jnp.dot(
            jnp.where(mask, 1.0, 0.0).astype(jnp.bfloat16), upto, preferred_element_type=jnp.float32
        )
        base = lax.broadcasted_iota(jnp.int32, count.shape, 1) // block * (block // 2) - 1
        where_to = jnp.where(mask, count + base.astype(jnp.float32), -1.0)[0:1, :]
        slot_i = lax.broadcasted_iota(jnp.int32, (slots, span), 0).astype(jnp.float32)
        sel = jnp.where(slot_i == where_to, 1.0, 0.0).astype(jnp.bfloat16)
        sel_v[t] = sel
        wcol = jnp.sum(extra.astype(jnp.float32) * pick[0:1].astype(jnp.float32), axis=1, keepdims=True)
        wcol_v[t] = jnp.broadcast_to(2.5 * wcol, (span, 128))
        gate = jnp.zeros((slots, part), jnp.float32)
        upper = jnp.zeros((slots, part), jnp.float32)
        for q in range(4):
            rows = tile_v[slot, :, :, :, q * wide : q * wide + quarter].reshape(span, quarter)
            served = jnp.dot(sel, rows, preferred_element_type=jnp.float32).astype(jnp.bfloat16)
            w = pl.ds(q * quarter, quarter)
            gate = gate + jnp.dot(served, wg_v[w, :], preferred_element_type=jnp.float32)
            upper = upper + jnp.dot(served, wu_v[w, :], preferred_element_type=jnp.float32)
        act = gate / (1.0 + jnp.exp(-gate)) * upper
        hall[attn, t] = act.astype(jnp.bfloat16)
        return carry

    lax.fori_loop(0, TILES, gate_up, 0)

    half = [pl.ds(0, TILES // 2), pl.ds(TILES // 2, TILES // 2)]
    hops = [send(hall.at[attn, half[d]], relay.at[d], along_z[d]) for d in range(2)]
    to_core = [send(hall.at[attn], hall.at[attn], sibling)]
    swap_until(BETWEEN)
    far = []
    for d in range(2):
        hops[d].wait_recv()
        origin = (wrap(z - 1) if d == 0 else wrap(z + 1)) // 2 * 2 + core
        far.append(send(relay.at[d], hall.at[origin, half[d]], along_z[d]))
    swap_until(LATE)
    opposite = (1 - z_hi) * 2 + core
    for d in range(2):
        far[d].wait_recv()
        to_core.append(send(hall.at[opposite, half[d]], hall.at[opposite, half[d]], sibling))
    for copy in to_core:
        copy.wait_recv()

    def down(step, t, carry):
        total = jnp.zeros((slots, quarter), jnp.float32)
        for a in range(4):
            total = total + jnp.dot(
                hall[a, t], wd_v[pl.ds(a * part, part), :], preferred_element_type=jnp.float32
            )
        produced = total.astype(jnp.bfloat16)
        spread = lax.dot_general(
            sel_v[t], produced, (((0,), (0,)), ((), ())), preferred_element_type=jnp.float32
        )
        scaled = (wcol_v[t][:, 0:1] * spread).astype(jnp.bfloat16)
        scaled = scaled.reshape(2, RING, block, quarter)
        low = lax.rem(t // 2, 2)
        for k in range(2):
            row = lax.rem(t, 2) * 2 + k
            if step == 0:
                tile_v[0, low, :, :, pl.ds(pl.multiple_of(row * quarter, 128), quarter)] = scaled[k]
            else:
                for i in range(RING):
                    tile_v[1, low, row, :, i * quarter : (i + 1) * quarter] = scaled[k, i]
        return carry

    for step in range(STEPS):
        lax.fori_loop(step * TILES // 2, (step + 1) * TILES // 2, functools.partial(down, step), 0)

    flow = (("y", "x"), ("x", "y"))

    def lane(step, at):
        return tile_v.at[step, :, :, :, pl.ds(pl.multiple_of(at * quarter, 128), quarter)]

    hops, fulls = {}, {}
    for s in range(STEPS):
        axis = flow[s][0]
        at = spot_on[axis]
        hops[s] = [send(lane(s, wrap(at + 2)).at[d], hop0.at[s, d], along[axis][d]) for d in range(2)]
    for s in range(STEPS):
        axis = flow[s][0]
        at = spot_on[axis]
        for d in range(2):
            target = wrap(at + 1) if d == 0 else wrap(at - 1)
            fulls[s, d] = [send(lane(s, target).at[1 - d], got0.at[s, d, 1 - d], along[axis][d])]
    for s in range(STEPS):
        axis = flow[s][0]
        at = spot_on[axis]
        for d in range(2):
            target = wrap(at + 1) if d == 0 else wrap(at - 1)
            hops[s][d].wait_recv()
            mine = lane(s, target)

            @pl.loop(0, RING)
            def _(i, mine=mine, s=s, d=d):
                total = mine[d, i].astype(jnp.float32) + hop0[s, d, i].astype(jnp.float32)
                hop0[s, d, i] = total.astype(jnp.bfloat16)

            fulls[s, d].append(send(hop0.at[s, d], got0.at[s, d, d], along[axis][d]))
    hops1, fulls1 = {}, {}
    for s in range(STEPS):
        at = spot_on[flow[s][0]]
        mine = lane(s, at)
        for d in range(2):
            for copy in fulls[s, d]:
                copy.wait_recv()

        @pl.loop(0, RING)
        def _(i, mine=mine, s=s):
            for h in range(2):
                total = mine[h, i].astype(jnp.float32)
                total = total + got0[s, 0, h, i].astype(jnp.float32)
                total = total + got0[s, 1, h, i].astype(jnp.float32)
                sum0[s, h, i] = total

        axis = flow[s][1]
        at = spot_on[axis]
        hops1[s] = [send(sum0.at[s, d, wrap(at + 2)], hop1.at[s, d], along[axis][d]) for d in range(2)]
    for s in range(STEPS):
        axis = flow[s][1]
        at = spot_on[axis]
        for d in range(2):
            target = wrap(at + 1) if d == 0 else wrap(at - 1)
            hops1[s][d].wait_recv()
            sum0[s, d, target] = sum0[s, d, target] + hop1[s, d]
            fulls1[s, d] = send(sum0.at[s, :, target], got1.at[s, d], along[axis][d])
    finals = []
    for s in range(STEPS):
        at = spot_on[flow[s][1]]
        for d in range(2):
            fulls1[s, d].wait_recv()
        away = 1 - z_lo
        sum1[s] = (sum0[s, away, at] + got1[s, 0, away] + got1[s, 1, away]).astype(jnp.bfloat16)
        finals.append(send(sum1.at[s], last.at[s], partner))
    swap_until(3 * PIECES)

    flag = swapped_ref[lax.rem(lax.axis_index("exp"), swapped_ref.shape[0])]
    settled = [0]

    def settle(count):
        while settled[0] < count:
            n = settled[0]
            dst, src = ((og_ref, wg_v), (ou_ref, wu_v), (od_ref, wd_v))[n // PIECES]
            size = src.shape[0] // PIECES
            start = n % PIECES * size
            swaps[n].wait_recv()

            @pl.loop(0, size // SLAB)
            def _(i, dst=dst, src=src, start=start):
                at = pl.ds(pl.multiple_of(start + i * SLAB, SLAB), SLAB)
                trade = jnp.full((SLAB, src.shape[1]), flag, jnp.int32) == 1
                dst[at, :] = jnp.where(trade, dst[at, :], src[at, :])

            settled[0] += 1

    settle(LATE - 2)
    for s in range(STEPS):
        at = spot_on[flow[s][1]]
        finals[s].wait_recv()
        total = sum0[s, z_lo, at] + got1[s, 0, z_lo] + got1[s, 1, z_lo] + last[s].astype(jnp.float32)
        mixed_ref[s] = total.astype(jnp.bfloat16)
    settle(3 * PIECES)
    for copy in send.copies + swaps:
        copy.wait_send()


def layer(held, swapped, tokens, logits, routes, w_gate, w_up, w_down):
    steps, rows, quarter = tokens.shape
    wide = quarter + EXTRA
    dt = tokens.dtype
    part = w_gate.shape[1]
    plane = (2, RING, RING, rows)
    hbm = pl.BlockSpec(memory_space=pl.ANY)
    vmem = pl.BlockSpec(memory_space=pltpu.VMEM)
    like = lambda a: jax.ShapeDtypeStruct(a.shape, a.dtype)
    return pl.pallas_call(
        layer_kernel,
        out_shape=(
            jax.ShapeDtypeStruct((steps, rows, quarter), dt),
            like(w_gate),
            like(w_up),
            like(w_down),
            jax.ShapeDtypeStruct((steps, *plane, 4 * wide), dt),
        ),
        in_specs=[*[pl.BlockSpec(memory_space=pltpu.HBM)] * 5, hbm, hbm, hbm],
        out_specs=(vmem, vmem, vmem, vmem, hbm),
        scratch_shapes=[
            pltpu.VMEM(w_gate.shape, dt),
            pltpu.VMEM(w_up.shape, dt),
            pltpu.VMEM(w_down.shape, dt),
            pltpu.SMEM(held.shape, held.dtype),
            pltpu.SMEM(swapped.shape, swapped.dtype),
            pltpu.VMEM(logits.shape, logits.dtype),
            pltpu.VMEM(routes.shape, routes.dtype),
            pltpu.VMEM((steps, rows, wide), dt),
            pltpu.VMEM((2, 2, RING, rows, 4 * wide), dt),
            pltpu.VMEM((4, TILES, 4 * rows, part), dt),
            pltpu.VMEM((2, TILES // 2, 4 * rows, part), dt),
            pltpu.VMEM((TILES, 4 * rows, 8 * rows), dt),
            pltpu.VMEM((TILES, 8 * rows, 128), jnp.float32),
            pltpu.VMEM((steps, 2, RING, rows, quarter), dt),
            pltpu.VMEM((steps, 2, 2, RING, rows, quarter), dt),
            pltpu.VMEM((steps, 2, RING, rows, quarter), jnp.float32),
            pltpu.VMEM((steps, 2, rows, quarter), jnp.float32),
            pltpu.VMEM((steps, 2, 2, rows, quarter), jnp.float32),
            pltpu.VMEM((steps, rows, quarter), dt),
            pltpu.VMEM((steps, rows, quarter), dt),
            pltpu.SemaphoreType.DMA((10,)),
            pltpu.SemaphoreType.DMA((2,)),
            pltpu.SemaphoreType.DMA((COPIES,)),
            pltpu.SemaphoreType.DMA((COPIES,)),
            pltpu.SemaphoreType.DMA((3 * PIECES,)),
            pltpu.SemaphoreType.DMA((3 * PIECES,)),
        ],
        compiler_params=pltpu.CompilerParams(
            collective_id=0, has_side_effects=True, vmem_limit_bytes=42 * 1024 * 1024
        ),
        name="layer",
    )(held, swapped, tokens, logits, routes, w_gate, w_up, w_down)[:4]


STORES = 2


def store_kernel(*refs):
    count = (len(refs) - 1) // 2
    sems = refs[-1]
    copies = []
    for k in range(count):
        src, dst = refs[k], refs[count + k]
        size = src.shape[0] // STORES
        for i in range(STORES):
            rows = pl.ds(i * size, size)
            copies.append(pltpu.make_async_copy(src.at[rows], dst.at[rows], sems.at[len(copies)]))
    for copy in copies:
        copy.start()
    for copy in copies:
        copy.wait()


def store(*arrays):
    return pl.pallas_call(
        store_kernel,
        out_shape=tuple(jax.ShapeDtypeStruct(a.shape, a.dtype) for a in arrays),
        in_specs=[pl.BlockSpec(memory_space=pltpu.VMEM)] * len(arrays),
        out_specs=(pl.BlockSpec(memory_space=pl.ANY),) * len(arrays),
        scratch_shapes=[pltpu.SemaphoreType.DMA((STORES * len(arrays),))],
        compiler_params=pltpu.CompilerParams(vmem_limit_bytes=16 * 1024 * 1024),
        name="store",
    )(*arrays)


def per_device(tokens, logits, routes, held, swapped, w_gate, w_up, w_down):
    by_choice = (jnp.swapaxes(logits, 1, 2), jnp.swapaxes(routes, 1, 2))
    held, swapped, tokens, *by_choice = (
        pltpu.with_memory_space_constraint(a, pltpu.HBM) for a in (held, swapped, tokens, *by_choice)
    )
    mixed, *tiles = layer(held, swapped, tokens, *by_choice, w_gate[0], w_up[0], w_down[0])
    mixed, *tiles = store(mixed, *tiles)
    return (mixed, *(tile[None] for tile in tiles))


def solution(mesh):
    in_specs = (
        P(None, "exp", "attn"),
        P(None, "exp", None),
        P(None, "exp", None),
        P(),
        P(),
        P("exp", None, "attn"),
        P("exp", None, "attn"),
        P("exp", None, "attn"),
    )
    out_specs = (
        P(None, "exp", "attn"),
        P("exp", None, "attn"),
        P("exp", None, "attn"),
        P("exp", None, "attn"),
    )
    return jax.shard_map(
        per_device, mesh=mesh, in_specs=in_specs, out_specs=out_specs, check_vma=False
    )
```
